32 devices in a mesh: section: 2 (over core), dp: 4 (over y, x), ctx: 4 (over z).
Axes of the slice: x: 2, y: 2, z: 4, core: 2. Of those that a mesh axis runs over, the one named last changes fastest.
Arguments:
- tokens: bfloat16 [2, 8, 1024, 768], P(None, 'dp', 'ctx'), may hold values from -6 to 6
- upstream: bfloat16 [2, 8, 1024, 768], P(None, 'dp', 'ctx'), may hold values from -6 to 6
- lengths: int32 [2, 8], P(None, 'dp'), may hold values from 512 to 1024, as said below
- w_qkv: float32 [2, 768, 2304], P('section', ('dp', 'ctx')), may hold values from -0.21875 to 0.21875
- w_out: float32 [2, 768, 768], P('section', ('dp', 'ctx')), may hold values from -4 to 4
- w_in: float32 [2, 768, 3072], P('section', ('dp', 'ctx')), may hold values from -0.21875 to 0.21875
- w_back: float32 [2, 3072, 768], P('section', ('dp', 'ctx')), may hold values from -0.109375 to 0.109375
- gain_attn: float32 [2, 768], P('section', ('dp', 'ctx')), may hold values from 0.1 to 1.9
- gain_ffn: float32 [2, 768], P('section', ('dp', 'ctx')), may hold values from 0.1 to 1.9
Outputs:
- acts: float32 [2, 2, 8, 1024, 768], P('section', None, 'dp', 'ctx')
- grads: float32 [2, 2, 8, 1024, 768], P('section', None, 'dp', 'ctx')
- grad_qkv: float32 [2, 768, 2304], P('section', ('dp', 'ctx'))
- grad_out: float32 [2, 768, 768], P('section', ('dp', 'ctx'))
- grad_in: float32 [2, 768, 3072], P('section', ('dp', 'ctx'))
- grad_back: float32 [2, 3072, 768], P('section', ('dp', 'ctx'))
- grad_gain_attn: float32 [2, 768], P('section', ('dp', 'ctx'))
- grad_gain_ffn: float32 [2, 768], P('section', ('dp', 'ctx'))
The draws below stay inside these ranges and needn't reach their ends.
Inputs may be any that keep to these rules, and one draw needn't show every extreme that they name: `lengths`: the number of real codons of each sequence, from 512 to 1024; some sequence has exactly 1024 and some exactly 512.
All inputs are finite; a program needn't handle non-finite values.
Results may differ from the reference program's by a relative error of at most 0.038.
Values may be sent and summed in bfloat16 or wider, within the bound.
No kernel may reach another device: no remote copies, remote signals or barrier semaphores. Data moves between devices by JAX's collectives and lax.ppermute only.
A program may use at most 320 MiB of HBM per device.

```python
import jax
import jax.numpy as jnp
from jax import lax

D = 768
HD = 64
FF = 3072
LEN = 1024
MB = 2
SEQ_MB = 2
SEQS = 8
N_SECTION = 2
N_DP = 4


def draw_lengths(key, part):
    entries = MB * SEQS
    values = jax.random.randint(key, (entries,), LEN // 2, LEN + 1)
    chosen = jax.random.randint(jax.random.fold_in(key, 7), (), 0, entries)
    values = values.at[chosen].set(LEN)
    values = values.at[(chosen + 1) % entries].set(LEN // 2)
    return values.reshape(MB, SEQS).astype(jnp.int32)


def levels(key, dims, cuts, smallest, largest):
    def one(dim, shards_of):
        steps = jax.random.uniform(jax.random.fold_in(jax.random.fold_in(key, 6), dim), (shards_of,), jnp.float32, smallest / len(cuts), largest / len(cuts))
        return jnp.repeat(jnp.exp(steps), dims[dim] // shards_of).reshape((-1,) + (1,) * (len(dims) - dim - 1))

    gain = one(*cuts[0])
    for cut in cuts[1:]:
        gain = gain * one(*cut)
    return gain


def scatter_about(own_key, shape, scale, bound, cuts=(), dtype=jnp.bfloat16):
    values = scale * jax.random.normal(own_key, shape, jnp.float32)
    if cuts:
        values = values * levels(own_key, shape, cuts, -0.22, 0.18)
    return jnp.clip(values, -bound, bound).astype(dtype)


def setup_inputs(seed: int = 0) -> dict:
    streams_of = jax.random.split(jax.random.key(seed), 10)
    return {
        "tokens": scatter_about(streams_of[0], (MB, SEQS, LEN, D), 1.0, 6.0, ((1, 4), (2, 4))),
        "upstream": scatter_about(streams_of[1], (MB, SEQS, LEN, D), 1.0, 6.0, ((1, 4), (2, 4))),
        "lengths": draw_lengths(jax.random.fold_in(streams_of[9], 71), 0),
        "w_qkv": scatter_about(streams_of[3], (N_SECTION, D, 3 * D), D ** -0.5, 0.21875, ((0, 2), (1, 16)), jnp.float32),
        "w_out": scatter_about(streams_of[4], (N_SECTION, D, D), (max(1, 3 * D // LEN)) ** -0.5, 4.0, ((0, 2), (1, 16)), jnp.float32),
        "w_in": scatter_about(streams_of[5], (N_SECTION, D, FF), D ** -0.5, 0.21875, ((0, 2), (1, 16)), jnp.float32),
        "w_back": scatter_about(streams_of[6], (N_SECTION, FF, D), FF ** -0.5, 0.109375, ((0, 2), (1, 16)), jnp.float32),
        "gain_attn": jnp.clip(1.0 + 0.18 * jax.random.normal(streams_of[7], (N_SECTION, D), jnp.float32), 0.1, 1.9),
        "gain_ffn": jnp.clip(1.0 + 0.18 * jax.random.normal(streams_of[8], (N_SECTION, D), jnp.float32), 0.1, 1.9),
    }


PRECISION_HIGHEST = lax.Precision.HIGHEST

@jax.custom_vjp
def low(v):
    return lax.optimization_barrier(v.astype(jnp.bfloat16)).astype(jnp.float32)

@jax.custom_vjp
def reduced_back_weight(v):
    return v

def low_keep(v):
    return (low(v), None)

def low_pass(kept, grad):
    return (grad,)

def back_keep(v):
    return (v, None)

def back_low(kept, grad):
    return (low(grad),)
low.defvjp(low_keep, low_pass)
reduced_back_weight.defvjp(back_keep, back_low)

def tables(positions):
    half_width = HD // 2
    frequency = jnp.power(10000.0, -(jnp.arange(half_width).astype(jnp.float32) * 2.0) / HD)
    angles = positions[:, None] * frequency[None, :]
    angles = jnp.concatenate([angles, angles], axis=1)
    return (jnp.cos(angles)[:, None, :], jnp.sin(angles)[:, None, :])

def rotate(tensor, cosine_tab, sine_tab):
    half_width = tensor.shape[-1] // 2
    turned = jnp.concatenate([-tensor[..., half_width:], tensor[..., :half_width]], axis=-1)
    return tensor * cosine_tab + turned * sine_tab

def layer_norm(residual_state, gain_vec):
    centred = residual_state - lax.optimization_barrier(jnp.mean(residual_state, axis=-1, keepdims=True))
    spread = lax.optimization_barrier(jnp.mean(centred * centred, axis=-1, keepdims=True))
    return centred * lax.rsqrt(spread + 1e-05) * gain_vec

def attend_pack(packed):
    query, key_rows, value_rows, length_one = packed
    scores = reduced_back_weight(jnp.einsum('qhd,khd->hqk', query, key_rows, precision=PRECISION_HIGHEST))
    key_mask = jnp.arange(LEN) < length_one
    scores = jnp.where(key_mask[None, None, :], scores, -1e+30)
    probabilities = low(jax.nn.softmax(scores, axis=-1))
    return jnp.einsum('hqk,khd->qhd', probabilities, value_rows, precision=PRECISION_HIGHEST)

def encoder_layer(residual_state, lengths_blk, params):
    query_key_value_matrix, output_weight_matrix, input_weight_matrix, back_weight_matrix, gain_one, gain_two = [low(master) for master in params]
    seq_total = residual_state.shape[0]
    head_count = D // HD
    cosine_tab, sine_tab = tables(jnp.arange(LEN).astype(jnp.float32))
    normed_input = low(layer_norm(residual_state, gain_one))
    query_key_value_rows = reduced_back_weight(jnp.einsum('aui,iv->auv', normed_input, query_key_value_matrix, precision=PRECISION_HIGHEST))
    query_key_value_rows = query_key_value_rows.reshape(seq_total, LEN, 3, head_count, HD)
    query = reduced_back_weight(low(rotate(query_key_value_rows[:, :, 0], cosine_tab, sine_tab) * HD ** (-0.5)))
    key_rows = reduced_back_weight(low(rotate(query_key_value_rows[:, :, 1], cosine_tab, sine_tab)))
    value_rows = low(query_key_value_rows[:, :, 2])
    attended_output = lax.map(jax.checkpoint(attend_pack), (query, key_rows, value_rows, lengths_blk))
    attended_output = reduced_back_weight(low(attended_output.reshape(seq_total, LEN, D)))
    middle_state = residual_state + reduced_back_weight(jnp.einsum('aui,iv->auv', attended_output, output_weight_matrix, precision=PRECISION_HIGHEST))
    normed_second = low(layer_norm(middle_state, gain_two))
    hidden_before_gelu = reduced_back_weight(jnp.einsum('wvz,zm->wvm', normed_second, input_weight_matrix, precision=PRECISION_HIGHEST))
    hidden_activation = low(jax.nn.gelu(hidden_before_gelu, approximate=False))
    return middle_state + reduced_back_weight(jnp.einsum('xvg,gt->xvt', hidden_activation, back_weight_matrix, precision=PRECISION_HIGHEST))

def reference(tokens, upstream, lengths, w_qkv, w_out, w_in, w_back, gain_attn, gain_ffn):
    masters = (w_qkv, w_out, w_in, w_back, gain_attn, gain_ffn)
    layer_params = [tuple((master[layer_id] for master in masters)) for layer_id in range(N_SECTION)]
    groups = MB * N_DP
    stream_in = tokens.astype(jnp.float32).reshape(groups, SEQ_MB, LEN, D)
    cotangent = upstream.astype(jnp.float32).reshape(groups, SEQ_MB, LEN, D)
    lengths_all = lengths.reshape(groups, SEQ_MB)
    zero_grads = tuple((tuple((jnp.zeros_like(master[0]) for master in masters)) for layer_id in range(N_SECTION)))

    def scan_step(running, packed):
        block_in, block_cot, block_len = packed
        outputs = []
        back_fns = []
        current = block_in
        for layer_id in range(N_SECTION):
            current, back_fn = jax.vjp(lambda residual_state, params: encoder_layer(residual_state, block_len, params), current, layer_params[layer_id])
            outputs.append(current)
            back_fns.append(back_fn)
        grad_now = block_cot
        grads_in = [None] * N_SECTION
        new_running = list(running)
        for layer_id in reversed(range(N_SECTION)):
            grad_now, grad_params = back_fns[layer_id](grad_now)
            grads_in[layer_id] = grad_now
            new_running[layer_id] = jax.tree.map(jnp.add, running[layer_id], grad_params)
        return (tuple(new_running), (jnp.stack(outputs), jnp.stack(grads_in)))
    totals, (outputs, grads_in) = lax.scan(scan_step, zero_grads, (stream_in, cotangent, lengths_all))
    acts = jnp.moveaxis(outputs, 1, 0).reshape(N_SECTION, MB, SEQS, LEN, D)
    grads = jnp.moveaxis(grads_in, 1, 0).reshape(N_SECTION, MB, SEQS, LEN, D)
    stacked = [jnp.stack([totals[layer_id][member] for layer_id in range(N_SECTION)]) for member in range(6)]
    return (acts, grads, stacked[0], stacked[1], stacked[2], stacked[3], stacked[4], stacked[5])
```

```python
import functools

import jax
import jax.numpy as jnp
from jax import lax
from jax.experimental import pallas as pl
from jax.experimental.pallas import tpu as pltpu
from jax.sharding import PartitionSpec as P

HD = 64
PAIR = 2 * HD
BF16 = jnp.bfloat16
F32 = jnp.float32
MASKED = -1e30
VMEM_LIMIT = 56 * 1024 * 1024


def nn(left, right):
    return lax.dot_general(left, right, (((1,), (0,)), ((), ())), preferred_element_type=F32)


def nt(left, right):
    return lax.dot_general(left, right, (((1,), (1,)), ((), ())), preferred_element_type=F32)


def tn(left, right):
    return lax.dot_general(left, right, (((0,), (0,)), ((), ())), preferred_element_type=F32)


def normalise(rows):
    centred = rows - jnp.mean(rows, axis=-1, keepdims=True)
    scale = lax.rsqrt(jnp.mean(centred * centred, axis=-1, keepdims=True) + 1e-05)
    return centred * scale, scale


def norm_back(rows, gain, grad):
    normed, scale = normalise(rows)
    inner = grad * gain
    mean_inner = jnp.mean(inner, axis=-1, keepdims=True)
    mean_along = jnp.mean(inner * normed, axis=-1, keepdims=True)
    grad_rows = scale * (inner - mean_inner - normed * mean_along)
    return grad_rows, jnp.sum(grad * normed, axis=0, keepdims=True)


def swap_halves(pair_block):
    lane = lax.broadcasted_iota(jnp.int32, pair_block.shape, 1)
    ahead = pltpu.roll(pair_block, PAIR - HD // 2, 1)
    behind = pltpu.roll(pair_block, HD // 2, 1)
    return jnp.where(lane % HD < HD // 2, ahead, behind)


class Plan:
    def __init__(self, tokens, w_in):
        micro, seqs, span, width = tokens.shape
        self.width = width
        self.hidden = w_in.shape[-1]
        self.heads = width // HD
        self.pairs = width // PAIR
        self.n_ctx = lax.axis_size("ctx")
        self.n_dp = lax.axis_size("dp")
        self.micro, self.seqs, self.span = micro, seqs, span
        self.n_seq = micro * seqs
        self.parts = self.n_ctx // self.n_seq
        assert self.parts * self.n_seq == self.n_ctx
        self.half = span // 2
        self.sub = self.half // self.parts
        self.rows = self.n_ctx * self.sub
        self.dp_bits = self.n_dp.bit_length() - 1
        assert 1 << self.dp_bits == self.n_dp
        self.section = lax.axis_index("section")
        self.dp = lax.axis_index("dp")
        self.ctx = lax.axis_index("ctx")
        shard = w_in.shape[1]
        self.direct = shard % 16 == 0 and self.n_ctx == 4
        self.pieces_z = self.n_ctx if self.direct else 1
        self.meta = jnp.stack([self.section, self.dp, self.ctx]).astype(jnp.int32)


def other_core(value):
    return lax.ppermute(value, "section", [(0, 1), (1, 0)])


def xor_dp(plan, value, bit):
    return lax.ppermute(value, "dp", [(i, i ^ (1 << bit)) for i in range(plan.n_dp)])


def xor_ctx(plan, value, mask):
    return lax.ppermute(value, "ctx", [(i, i ^ mask) for i in range(plan.n_ctx)])


def spread_ctx(plan, shard):
    if plan.direct:
        parts = [shard] + [xor_ctx(plan, shard, d) for d in range(1, plan.n_ctx)]
        return jnp.concatenate(parts, axis=0)
    return lax.all_gather(shard, "ctx", axis=0, tiled=True)


def spread(plan, shard, low_first):
    pieces = {0: spread_ctx(plan, shard)}
    bits = range(plan.dp_bits) if low_first else reversed(range(plan.dp_bits))
    for bit in bits:
        for mask in list(pieces):
            pieces[mask | (1 << bit)] = xor_dp(plan, pieces[mask], bit)
    own = [pieces[mask] for mask in range(plan.n_dp)]
    return own, [other_core(piece) for piece in own]


def collect(plan, pieces, low_first):
    pieces = dict(enumerate(pieces))
    bits = list(range(plan.dp_bits)) if low_first else list(reversed(range(plan.dp_bits)))
    for bit in bits:
        kept = [mask for mask in pieces if not mask & (1 << bit)]
        got = {mask: xor_dp(plan, pieces[mask | (1 << bit)], bit) for mask in kept}
        pieces = {
            mask: (pieces[mask].astype(F32) + got[mask].astype(F32)).astype(BF16) for mask in kept
        }
    block = pieces[0]
    if plan.direct:
        size = block.shape[0] // plan.n_ctx
        parts = [block[d * size : (d + 1) * size] for d in range(plan.n_ctx)]
        total = parts[0].astype(F32)
        for d in range(1, plan.n_ctx):
            total = total + xor_ctx(plan, parts[d], d).astype(F32)
        return total.astype(BF16)
    return lax.psum_scatter(block, "ctx", scatter_dimension=0, tiled=True)


def smem():
    return pl.BlockSpec(memory_space=pltpu.SMEM)


def vmem():
    return pl.BlockSpec(memory_space=pltpu.VMEM)


def anywhere():
    return pl.BlockSpec(memory_space=pl.ANY)


def params(**kw):
    return pltpu.CompilerParams(vmem_limit_bytes=VMEM_LIMIT, **kw)


def cost(flops, bytes_accessed, transcendentals=0):
    return pl.CostEstimate(
        flops=int(flops), bytes_accessed=int(bytes_accessed), transcendentals=int(transcendentals)
    )


def block_starts(meta, n_dp, n_z, block):
    size = block // n_z
    for mask in range(n_dp):
        for d in range(n_z):
            start = (meta[1] ^ mask) * block
            if n_z > 1:
                start = start + (meta[2] ^ d) * size
            yield mask, d * size, start, size


def piece_copies(meta, refs, place, sems, first, n_z):
    copies = []
    block = refs[0].shape[0]
    for mask, row, start, size in block_starts(meta, len(refs), n_z, block):
        start = pl.multiple_of(start, 16)
        copies.append(
            pltpu.make_async_copy(
                refs[mask].at[pl.ds(row, size), :],
                place(start, size),
                sems.at[first + len(copies)],
            )
        )
    return copies


def run(copies):
    for copy in copies:
        copy.start()


def wait(copies):
    for copy in copies:
        copy.wait()


def qkv_kernel(n_dp, n_z, meta, x_ref, gain_ref, cos_ref, sin_ref, *refs):
    qk_own, qk_other, vo_own, vo_other = (refs[i * n_dp : (i + 1) * n_dp] for i in range(4))
    a_ref, q_ref, kv_ref, wqk, wv, sems = refs[4 * n_dp :]
    section = meta[0]
    count = n_dp * n_z

    def at_half(which):
        return lambda start, size: wqk.at[which, pl.ds(start, size), :]

    def at_v(start, size):
        return wv.at[pl.ds(start, size), :]

    qk = piece_copies(meta, qk_own, at_half(section), sems, 0, n_z)
    qk += piece_copies(meta, qk_other, at_half(1 - section), sems, count, n_z)
    run(qk)
    v_own = piece_copies(meta, vo_own, at_v, sems, 2 * count, n_z)
    v_other = piece_copies(meta, vo_other, at_v, sems, 2 * count, n_z)

    @pl.when(section == 0)
    def _():
        run(v_own)

    @pl.when(section != 0)
    def _():
        run(v_other)

    normed, _ = normalise(x_ref[...])
    a_ref[...] = (normed * gain_ref[...]).astype(BF16)
    wait(qk)

    @pl.when(section == 0)
    def _():
        wait(v_own)

    @pl.when(section != 0)
    def _():
        wait(v_other)

    rows, width = a_ref.shape
    step = 256 if rows % 256 == 0 else rows

    def body(i, carry):
        at = pl.ds(pl.multiple_of(i * step, step), step)
        a = a_ref[at, :]
        cos, sin = cos_ref[at, :], sin_ref[at, :]
        for which in range(2):
            out = nn(a, wqk[which])
            for pair in range(width // PAIR):
                lanes = slice(pair * PAIR, (pair + 1) * PAIR)
                block = out[:, lanes]
                turned = block * cos + swap_halves(block) * sin
                if which == 0:
                    q_ref[at, lanes] = (turned * HD**-0.5).astype(BF16)
                else:
                    kv_ref[0, at, lanes] = turned.astype(BF16)
        kv_ref[1, at, :] = nn(a, wv[...]).astype(BF16)
        return carry

    lax.fori_loop(0, rows // step, body, 0)


def qkv_forward(plan, x, gain, cos, sin, qk, vo):
    rows, width = x.shape
    n = plan.n_dp
    count = n * plan.pieces_z
    return pl.pallas_call(
        functools.partial(qkv_kernel, n, plan.pieces_z),
        out_shape=[
            jax.ShapeDtypeStruct((rows, width), BF16),
            jax.ShapeDtypeStruct((rows, width), BF16),
            jax.ShapeDtypeStruct((2, rows, width), BF16),
        ],
        in_specs=[smem(), vmem(), vmem(), vmem(), vmem()] + [anywhere()] * (4 * n),
        out_specs=[vmem(), vmem(), vmem()],
        scratch_shapes=[
            pltpu.VMEM((2, width, width), BF16),
            pltpu.VMEM((width, width), BF16),
            pltpu.SemaphoreType.DMA((3 * count,)),
        ],
        compiler_params=params(),
        cost_estimate=cost(6 * rows * width * width, 12 * rows * width + 6 * width * width),
        name="qkv_forward",
    )(plan.meta, x, gain, cos, sin, *qk[0], *qk[1], *vo[0], *vo[1])


def lane_mask(shape, head):
    lane = lax.broadcasted_iota(jnp.int32, shape, 1)
    return lane < HD if head == 0 else lane >= HD


def with_ones(query):
    lane = lax.broadcasted_iota(jnp.int32, query.shape, 1)
    return jnp.concatenate([query, jnp.where(lane == 0, 1.0, 0.0).astype(BF16)], axis=1)


def attention_kernel(chunks, key_block, q_ref, *refs):
    kv = refs[:chunks]
    bias_ref, o_ref, lse_ref, s_scr, vt_scr = refs[chunks:]
    rows = q_ref.shape[0]
    per_chunk = rows // key_block
    query = q_ref[...]
    for c in range(chunks):
        vt_scr[:, c * rows : (c + 1) * rows] = jnp.transpose(kv[c][1])
    outs = []
    for head in range(2):
        extended = with_ones(jnp.where(lane_mask(query.shape, head), query, jnp.zeros_like(query)))
        peak = jnp.full((1, rows), -jnp.inf, F32)
        for c in range(chunks):
            for j in range(per_chunk):
                at = slice(j * key_block, (j + 1) * key_block)
                everywhere = slice(c * rows + at.start, c * rows + at.stop)
                keys = jnp.concatenate([kv[c][0, at, :], bias_ref[everywhere, :]], axis=1)
                scores = nt(keys, extended)
                s_scr[everywhere, :] = scores
                peak = jnp.maximum(peak, jnp.max(scores, axis=0, keepdims=True))
        total = jnp.zeros((1, rows), F32)
        out = jnp.zeros((PAIR, rows), F32)
        for c in range(chunks):
            for j in range(per_chunk):
                everywhere = slice(c * rows + j * key_block, c * rows + (j + 1) * key_block)
                weights = jnp.exp(s_scr[everywhere, :] - peak)
                total = total + jnp.sum(weights, axis=0, keepdims=True)
                out = out + nn(vt_scr[:, everywhere], weights.astype(BF16))
        lse_ref[0, head : head + 1, :] = peak + jnp.log(total)
        outs.append(out / total)
    row = lax.broadcasted_iota(jnp.int32, outs[0].shape, 0)
    o_ref[...] = jnp.transpose(jnp.where(row < HD, outs[0], outs[1])).astype(BF16)


def attention_forward(plan, query, kv, bias):
    rows, width = query.shape
    chunks = len(kv)
    keys = chunks * rows
    pair_block = pl.BlockSpec((rows, PAIR), lambda p: (0, p))
    kv_block = pl.BlockSpec((2, rows, PAIR), lambda p: (0, 0, p))
    return pl.pallas_call(
        functools.partial(attention_kernel, chunks, min(256, rows)),
        out_shape=[
            jax.ShapeDtypeStruct((rows, width), BF16),
            jax.ShapeDtypeStruct((plan.pairs, 8, rows), F32),
        ],
        grid=(plan.pairs,),
        in_specs=[pair_block] + [kv_block] * chunks + [pl.BlockSpec((keys, PAIR), lambda p: (0, 0))],
        out_specs=[pair_block, pl.BlockSpec((1, 8, rows), lambda p: (p, 0, 0))],
        scratch_shapes=[pltpu.VMEM((keys, rows), F32), pltpu.VMEM((PAIR, keys), BF16)],
        compiler_params=params(),
        cost_estimate=cost(
            16 * rows * keys * width, 4 * rows * width + 4 * keys * width, rows * keys * plan.heads
        ),
        name="attention_forward",
    )(query, *kv, bias)


def out_kernel(n_dp, n_z, meta, o_ref, x_ref, gain_ref, *refs):
    vo_own, vo_other = refs[:n_dp], refs[n_dp : 2 * n_dp]
    u2_ref, b_ref, wo, sems = refs[2 * n_dp :]
    section = meta[0]

    def at_o(start, size):
        return wo.at[pl.ds(start, size), :]

    own = piece_copies(meta, vo_own, at_o, sems, 0, n_z)
    other = piece_copies(meta, vo_other, at_o, sems, 0, n_z)

    @pl.when(section == 1)
    def _():
        run(own)
        wait(own)

    @pl.when(section != 1)
    def _():
        run(other)
        wait(other)

    rows = o_ref.shape[0]
    step = 256 if rows % 256 == 0 else rows

    def body(i, carry):
        at = pl.ds(pl.multiple_of(i * step, step), step)
        u2 = x_ref[at, :] + nn(o_ref[at, :], wo[...])
        u2_ref[at, :] = u2
        b_ref[at, :] = (normalise(u2)[0] * gain_ref[...]).astype(BF16)
        return carry

    lax.fori_loop(0, rows // step, body, 0)


def out_forward(plan, o, x, gain, vo):
    rows, width = x.shape
    n = plan.n_dp
    return pl.pallas_call(
        functools.partial(out_kernel, n, plan.pieces_z),
        out_shape=[
            jax.ShapeDtypeStruct((rows, width), F32),
            jax.ShapeDtypeStruct((rows, width), BF16),
        ],
        in_specs=[smem(), vmem(), vmem(), vmem()] + [anywhere()] * (2 * n),
        out_specs=[vmem(), vmem()],
        scratch_shapes=[
            pltpu.VMEM((width, width), BF16),
            pltpu.SemaphoreType.DMA((n * plan.pieces_z,)),
        ],
        compiler_params=params(),
        cost_estimate=cost(2 * rows * width * width, 12 * rows * width + 2 * width * width),
        name="out_forward",
    )(plan.meta, o, x, gain, *vo[0], *vo[1])


def ffn_copies(meta, n_z, w1_own, w1_other, w2_own, w2_other, w1, w2, sems):
    section = meta[0]
    half1 = w1.shape[1] // 2
    half2 = w2.shape[1] // 2
    count = len(w1_own) * n_z

    def at(matrix, which, half):
        lanes = pl.ds(pl.multiple_of(which * half, 128), half)
        return lambda start, size: matrix.at[pl.ds(start, size), lanes]

    first = piece_copies(meta, w1_own, at(w1, section, half1), sems, 0, n_z)
    first += piece_copies(meta, w1_other, at(w1, 1 - section, half1), sems, count, n_z)
    second = piece_copies(meta, w2_own, at(w2, section, half2), sems, 2 * count, n_z)
    second += piece_copies(meta, w2_other, at(w2, 1 - section, half2), sems, 3 * count, n_z)
    return first, second


def ffn_kernel(n_dp, n_z, chunk, meta, b_ref, u2_ref, *refs):
    w1_own, w1_other, w2_own, w2_other = (refs[i * n_dp : (i + 1) * n_dp] for i in range(4))
    acts_ref, low_ref, h_ref, slope_ref, w1, w2, sems = refs[4 * n_dp :]
    first, second = ffn_copies(meta, n_z, w1_own, w1_other, w2_own, w2_other, w1, w2, sems)
    run(first)
    run(second)
    acts_ref[...] = u2_ref[...]
    wait(first)
    wait(second)

    def body(i, carry):
        at = pl.ds(pl.multiple_of(i * chunk, chunk), chunk)
        hp = nn(b_ref[...], w1[:, at])
        cdf = 0.5 * (1.0 + lax.erf(hp * (0.5**0.5)))
        density = jnp.exp(-0.5 * hp * hp) * 0.3989422804014327
        h = (hp * cdf).astype(BF16)
        h_ref[:, at] = h
        slope_ref[:, at] = (cdf + hp * density).astype(BF16)
        acts_ref[...] += nn(h, w2[at, :])
        return carry

    lax.fori_loop(0, w1.shape[1] // chunk, body, 0)
    low_ref[...] = acts_ref[...].astype(BF16)


def ffn_forward(plan, b, u2, w1, w2):
    rows, width = u2.shape
    n, hidden = plan.n_dp, plan.hidden
    return pl.pallas_call(
        functools.partial(ffn_kernel, n, plan.pieces_z, 512),
        out_shape=[
            jax.ShapeDtypeStruct((rows, width), F32),
            jax.ShapeDtypeStruct((rows, width), BF16),
            jax.ShapeDtypeStruct((rows, hidden), BF16),
            jax.ShapeDtypeStruct((rows, hidden), BF16),
        ],
        in_specs=[smem(), vmem(), vmem()] + [anywhere()] * (4 * n),
        out_specs=[vmem()] * 4,
        scratch_shapes=[
            pltpu.VMEM((width, hidden), BF16),
            pltpu.VMEM((hidden, width), BF16),
            pltpu.SemaphoreType.DMA((4 * n * plan.pieces_z,)),
        ],
        compiler_params=params(),
        cost_estimate=cost(
            4 * rows * width * hidden + 60 * rows * hidden,
            12 * rows * width + 4 * rows * hidden + 4 * width * hidden,
            2 * rows * hidden,
        ),
        name="ffn_forward",
    )(plan.meta, b, u2, *w1[0], *w1[1], *w2[0], *w2[1])


def ffn_back_kernel(n_dp, n_z, chunk, meta, c_ref, slope_ref, u2_ref, gain_ref, *refs):
    w1_own, w1_other, w2_own, w2_other, vo_own, vo_other = (
        refs[i * n_dp : (i + 1) * n_dp] for i in range(6)
    )
    cf_ref, dhp_ref, du2_ref, dz_ref, do_ref, dg_ref, w1, w2, wo, acc, sems = refs[6 * n_dp :]
    section = meta[0]
    count = n_dp * n_z
    first, second = ffn_copies(meta, n_z, w1_own, w1_other, w2_own, w2_other, w1, w2, sems)
    run(second)
    run(first)

    def at_o(start, size):
        return wo.at[pl.ds(start, size), :]

    own = piece_copies(meta, vo_own, at_o, sems, 4 * count, n_z)
    other = piece_copies(meta, vo_other, at_o, sems, 4 * count, n_z)

    @pl.when(section == 1)
    def _():
        run(own)

    @pl.when(section != 1)
    def _():
        run(other)

    cf_ref[...] = c_ref[...].astype(BF16)
    acc[...] = jnp.zeros_like(acc)
    wait(second)
    wait(first)

    def body(i, carry):
        at = pl.ds(pl.multiple_of(i * chunk, chunk), chunk)
        dh = nt(cf_ref[...], w2[at, :])
        dhp = (dh * slope_ref[:, at].astype(F32)).astype(BF16)
        dhp_ref[:, at] = dhp
        acc[...] += nt(dhp, w1[:, at])
        return carry

    lax.fori_loop(0, w1.shape[1] // chunk, body, 0)

    @pl.when(section == 1)
    def _():
        wait(own)

    @pl.when(section != 1)
    def _():
        wait(other)

    grad, dgain = norm_back(u2_ref[...], gain_ref[...], acc[...])
    du2 = c_ref[...].astype(F32) + grad
    du2_ref[...] = du2
    dg_ref[...] = dgain
    dz = du2.astype(BF16)
    dz_ref[...] = dz
    do_ref[...] = nt(dz, wo[...]).astype(BF16)


def ffn_backward(plan, c, slope, u2, gain, w1, w2, vo):
    rows, width = u2.shape
    n, hidden = plan.n_dp, plan.hidden
    wide = jax.ShapeDtypeStruct((rows, width), BF16)
    return pl.pallas_call(
        functools.partial(ffn_back_kernel, n, plan.pieces_z, 512),
        out_shape=[
            wide,
            jax.ShapeDtypeStruct((rows, hidden), BF16),
            jax.ShapeDtypeStruct((rows, width), F32),
            wide,
            wide,
            jax.ShapeDtypeStruct((1, width), F32),
        ],
        in_specs=[smem()] + [vmem()] * 4 + [anywhere()] * (6 * n),
        out_specs=[vmem()] * 6,
        scratch_shapes=[
            pltpu.VMEM((width, hidden), BF16),
            pltpu.VMEM((hidden, width), BF16),
            pltpu.VMEM((width, width), BF16),
            pltpu.VMEM((rows, width), F32),
            pltpu.SemaphoreType.DMA((5 * n * plan.pieces_z,)),
        ],
        compiler_params=params(),
        cost_estimate=cost(
            4 * rows * width * hidden + 2 * rows * width * width,
            18 * rows * width + 4 * rows * hidden + 4 * width * hidden + 2 * width * width,
        ),
        name="ffn_backward",
    )(plan.meta, c, slope, u2, gain, *w1[0], *w1[1], *w2[0], *w2[1], *vo[0], *vo[1])


def attention_back_kernel(chunks, key_block, q_ref, do_ref, o_ref, lse_ref, bias_ref, *refs):
    kv = refs[:chunks]
    dq_ref, dk_ref, dv_ref = refs[chunks : chunks + 3]
    far = refs[chunks + 3 : 2 * chunks + 2]
    kt_scr, dk_scr, dv_scr = refs[2 * chunks + 2 :]
    rows = q_ref.shape[0]
    per_chunk = rows // key_block
    query, grad = q_ref[...], do_ref[...]
    for c in range(chunks):
        kt_scr[:, c * rows : (c + 1) * rows] = jnp.transpose(kv[c][0])
    products = jnp.transpose(grad.astype(F32) * o_ref[...].astype(F32))
    outs = []
    for head in range(2):
        mask = lane_mask(query.shape, head)
        masked_query = jnp.where(mask, query, jnp.zeros_like(query))
        masked_grad = jnp.where(mask, grad, jnp.zeros_like(grad))
        extended = with_ones(masked_query)
        delta = jnp.sum(products[head * HD : (head + 1) * HD], axis=0, keepdims=True)
        lse = lse_ref[0, head : head + 1, :]
        dqt = jnp.zeros((PAIR, rows), F32)
        for c in range(chunks):
            for j in range(per_chunk):
                at = slice(j * key_block, (j + 1) * key_block)
                everywhere = slice(c * rows + at.start, c * rows + at.stop)
                keys = jnp.concatenate([kv[c][0, at, :], bias_ref[everywhere, :]], axis=1)
                weights = jnp.exp(nt(keys, extended) - lse)
                grad_weights = nt(kv[c][1, at, :], masked_grad)
                grad_scores = (weights * (grad_weights - delta)).astype(BF16)
                dv = nn(weights.astype(BF16), masked_grad)
                dk = nn(grad_scores, masked_query)
                dqt = dqt + nn(kt_scr[:, everywhere], grad_scores)
                if head == 0:
                    dv_scr[everywhere, :] = dv
                    dk_scr[everywhere, :] = dk
                elif c == 0:
                    dk_ref[at, :] = dk_scr[everywhere, :] + dk
                    dv_ref[at, :] = dv_scr[everywhere, :] + dv
                else:
                    far[c - 1][0, at, :] = (dk_scr[everywhere, :] + dk).astype(BF16)
                    far[c - 1][1, at, :] = (dv_scr[everywhere, :] + dv).astype(BF16)
        outs.append(dqt)
    row = lax.broadcasted_iota(jnp.int32, outs[0].shape, 0)
    dq_ref[...] = jnp.transpose(jnp.where(row < HD, outs[0], outs[1])).astype(BF16)


def attention_backward(plan, query, grad, o, lse, bias, kv):
    rows, width = query.shape
    chunks = len(kv)
    keys = chunks * rows
    pair_block = pl.BlockSpec((rows, PAIR), lambda p: (0, p))
    kv_block = pl.BlockSpec((2, rows, PAIR), lambda p: (0, 0, p))
    near = jax.ShapeDtypeStruct((rows, width), F32)
    return pl.pallas_call(
        functools.partial(attention_back_kernel, chunks, min(256, rows)),
        out_shape=[jax.ShapeDtypeStruct((rows, width), BF16), near, near]
        + [jax.ShapeDtypeStruct((2, rows, width), BF16)] * (chunks - 1),
        grid=(plan.pairs,),
        in_specs=[pair_block] * 3
        + [
            pl.BlockSpec((1, 8, rows), lambda p: (p, 0, 0)),
            pl.BlockSpec((keys, PAIR), lambda p: (0, 0)),
        ]
        + [kv_block] * chunks,
        out_specs=[pair_block] * 3 + [kv_block] * (chunks - 1),
        scratch_shapes=[
            pltpu.VMEM((PAIR, keys), BF16),
            pltpu.VMEM((keys, PAIR), F32),
            pltpu.VMEM((keys, PAIR), F32),
        ],
        compiler_params=params(),
        cost_estimate=cost(
            40 * rows * keys * width,
            16 * rows * width + 8 * keys * width,
            rows * keys * plan.heads,
        ),
        name="attention_backward",
    )(query, grad, o, lse, bias, *kv)


def qkv_back_kernel(
    n_dp, n_z, n_far, meta, dq_ref, dk_ref, dv_ref, du2_ref, x_ref, gain_ref, cos_ref, sin_ref, *refs
):
    far = refs[:n_far]
    qk_own, qk_other, vo_own, vo_other = (
        refs[n_far + i * n_dp : n_far + (i + 1) * n_dp] for i in range(4)
    )
    dqkv_ref, dx_ref, low_ref, dg_ref, wqk, wv, sems = refs[n_far + 4 * n_dp :]
    section = meta[0]
    count = n_dp * n_z

    def at_half(which):
        return lambda start, size: wqk.at[which, pl.ds(start, size), :]

    def at_v(start, size):
        return wv.at[pl.ds(start, size), :]

    qk = piece_copies(meta, qk_own, at_half(section), sems, 0, n_z)
    qk += piece_copies(meta, qk_other, at_half(1 - section), sems, count, n_z)
    run(qk)
    v_own = piece_copies(meta, vo_own, at_v, sems, 2 * count, n_z)
    v_other = piece_copies(meta, vo_other, at_v, sems, 2 * count, n_z)

    @pl.when(section == 0)
    def _():
        run(v_own)

    @pl.when(section != 0)
    def _():
        run(v_other)

    rows, width = x_ref.shape
    cos, sin = cos_ref[...], sin_ref[...]
    for pair in range(width // PAIR):
        lanes = slice(pair * PAIR, (pair + 1) * PAIR)
        dq = dq_ref[:, lanes].astype(F32) * HD**-0.5
        dk, dv = dk_ref[:, lanes], dv_ref[:, lanes]
        for part in far:
            dk = dk + part[0, :, lanes].astype(F32)
            dv = dv + part[1, :, lanes].astype(F32)
        dk = dk.astype(BF16).astype(F32)
        dqkv_ref[:, pair * PAIR : (pair + 1) * PAIR] = (dq * cos - swap_halves(dq) * sin).astype(BF16)
        at = width + pair * PAIR
        dqkv_ref[:, at : at + PAIR] = (dk * cos - swap_halves(dk) * sin).astype(BF16)
        at = 2 * width + pair * PAIR
        dqkv_ref[:, at : at + PAIR] = dv.astype(BF16)
    wait(qk)

    @pl.when(section == 0)
    def _():
        wait(v_own)

    @pl.when(section != 0)
    def _():
        wait(v_other)

    da = nt(dqkv_ref[:, :width], wqk[0])
    da = da + nt(dqkv_ref[:, width : 2 * width], wqk[1])
    da = da + nt(dqkv_ref[:, 2 * width :], wv[...])
    grad, dgain = norm_back(x_ref[...], gain_ref[...], da)
    dx = du2_ref[...] + grad
    dx_ref[...] = dx
    low_ref[...] = dx.astype(BF16)
    dg_ref[...] = dgain


def qkv_backward(plan, dq, dk, dv, far, du2, x, gain, cos, sin, qk, vo):
    rows, width = x.shape
    n = plan.n_dp
    return pl.pallas_call(
        functools.partial(qkv_back_kernel, n, plan.pieces_z, len(far)),
        out_shape=[
            jax.ShapeDtypeStruct((rows, 3 * width), BF16),
            jax.ShapeDtypeStruct((rows, width), F32),
            jax.ShapeDtypeStruct((rows, width), BF16),
            jax.ShapeDtypeStruct((1, width), F32),
        ],
        in_specs=[smem()] + [vmem()] * (8 + len(far)) + [anywhere()] * (4 * n),
        out_specs=[vmem()] * 4,
        scratch_shapes=[
            pltpu.VMEM((2, width, width), BF16),
            pltpu.VMEM((width, width), BF16),
            pltpu.SemaphoreType.DMA((3 * n * plan.pieces_z,)),
        ],
        compiler_params=params(),
        cost_estimate=cost(6 * rows * width * width, 30 * rows * width + 6 * width * width),
        name="qkv_backward",
    )(plan.meta, dq, dk, dv, du2, x, gain, cos, sin, *far, *qk[0], *qk[1], *vo[0], *vo[1])


def weight_kernel(n_dp, n_z, mine, half, start, chunk, meta, left_ref, right_ref, *refs):
    if mine:
        got_ref, outs, acc = refs[0], refs[1:-1], refs[-1]
    else:
        got_ref, outs, acc = None, refs[:-1], refs[-1]
    cols = acc.shape[1]
    which = meta[0] if mine else 1 - meta[0]
    lanes = pl.ds(pl.multiple_of(which * half + start, 128), cols)

    def body(i, carry):
        at = pl.ds(pl.multiple_of(i * chunk, chunk), chunk)
        acc[at, :] = tn(left_ref[:, at], right_ref[:, lanes])
        return carry

    total = acc.shape[0]
    lax.fori_loop(0, total // chunk, body, 0)
    block = total // n_dp
    for mask, row, begin, size in block_starts(meta, n_dp, n_z, block):
        rows = acc[pl.ds(pl.multiple_of(begin, 8), size), :]
        at = slice(mask * block + row, mask * block + row + size)
        if mine:
            outs[mask][row : row + size, :] = (rows + got_ref[at, :].astype(F32)).astype(BF16)
        else:
            outs[0][at, :] = rows.astype(BF16)


def weight_half(plan, left, right, half, start, cols, got):
    rows, total = left.shape
    n = plan.n_dp
    mine = got is not None
    out = jax.ShapeDtypeStruct((total // n, cols), BF16)
    result = pl.pallas_call(
        functools.partial(weight_kernel, n, plan.pieces_z, mine, half, start, 256),
        out_shape=[out] * n if mine else [jax.ShapeDtypeStruct((total, cols), BF16)],
        in_specs=[smem(), vmem(), vmem()] + ([vmem()] if mine else []),
        out_specs=[vmem()] * (n if mine else 1),
        scratch_shapes=[pltpu.VMEM((total, cols), F32)],
        compiler_params=params(),
        cost_estimate=cost(
            2 * rows * total * cols, 2 * rows * (total + cols) + 2 * total * cols * (2 if mine else 1)
        ),
        name="weight_half",
    )(plan.meta, left, right, *([got] if mine else []))
    return result if mine else result[0]


def weight_grad(plan, left, right, cols, start, low_first):
    half = right.shape[1] // 2
    theirs = weight_half(plan, left, right, half, start, cols, None)
    pieces = weight_half(plan, left, right, half, start, cols, other_core(theirs))
    return collect(plan, pieces, low_first)


def by_section(plan, first, second):
    return jnp.where(plan.section == 0, first, second)


def take_half(plan, matrix, which):
    half = matrix.shape[-1] // 2
    return lax.dynamic_slice_in_dim(matrix, which * half, half, axis=matrix.ndim - 1)


def to_sequences(plan, tokens):
    pieces = tokens.reshape(plan.n_seq, 2, plan.half, plan.width)
    mine = lax.dynamic_index_in_dim(pieces, plan.section, 1, keepdims=False)
    mine = mine.reshape(plan.n_ctx, plan.sub, plan.width)
    moved = lax.all_to_all(mine, "ctx", 0, 0, tiled=True)
    return moved.reshape(plan.rows, plan.width)


def from_sequences(plan, rows):
    pieces = rows.reshape(plan.n_ctx, plan.sub, plan.width)
    moved = lax.all_to_all(pieces, "ctx", 0, 0, tiled=True)
    return moved.reshape(plan.n_seq, plan.half, plan.width)


def to_output(plan, layers):
    own = by_section(plan, layers[0], layers[1])
    got = other_core(by_section(plan, layers[1], layers[0]))
    first = by_section(plan, own, got)
    second = by_section(plan, got, own)
    both = jnp.stack([first, second], axis=1).astype(F32)
    return both.reshape(1, plan.micro, plan.seqs, plan.span, plan.width)


def gather_gains(plan, gain_attn, gain_ffn):
    own = jnp.stack([gain_attn[0], gain_ffn[0]]).astype(BF16)
    got = other_core(own)
    both = jnp.stack([by_section(plan, own, got), by_section(plan, got, own)])
    block = both.reshape(1, -1)
    parts = [block]
    for d in range(1, plan.n_ctx):
        parts.append(xor_ctx(plan, block, d))
    block = jnp.concatenate(parts, axis=0)
    for bit in range(plan.dp_bits):
        block = jnp.concatenate([block, xor_dp(plan, block, bit)], axis=0)
    total = plan.n_ctx * plan.n_dp
    place = jnp.arange(total)
    source = (((place // plan.n_ctx) ^ plan.dp) * plan.n_ctx) + ((place % plan.n_ctx) ^ plan.ctx)
    chosen = (jnp.arange(total)[:, None] == source[None, :]).astype(F32)
    ordered = jnp.dot(chosen, block.astype(F32), precision=lax.Precision.HIGHEST)
    gains = ordered.reshape(total, 2, 2, -1).transpose(1, 2, 0, 3).reshape(2, 2, 1, plan.width)
    return gains


def sum_gains(plan, gains):
    total = gains + other_core(gains)
    for bit in range(plan.dp_bits):
        total = total + xor_dp(plan, total, bit)
    mask = 1
    while mask < plan.n_ctx:
        total = total + xor_ctx(plan, total, mask)
        mask *= 2
    layer = lax.dynamic_slice_in_dim(total, plan.section * 2, 2, axis=0)
    size = plan.width // (plan.n_dp * plan.n_ctx)
    place = (plan.dp * plan.n_ctx + plan.ctx) * size
    mine = lax.dynamic_slice_in_dim(layer, place, size, axis=1)
    return mine[0:1], mine[1:2]


def shared_keys(plan, own):
    chunks = []
    for mask in range(plan.parts):
        here = own if mask == 0 else xor_ctx(plan, own, mask)
        chunks += [here, other_core(here)]
    return chunks


def return_keys(plan, far):
    got = []
    for mask in range(plan.parts):
        for core in range(2):
            index = 2 * mask + core
            if index == 0:
                continue
            part = far[index - 1]
            if core:
                part = other_core(part)
            if mask:
                part = xor_ctx(plan, part, mask)
            got.append(part)
    return got


def positions_of(plan, section, ctx):
    part = ctx % plan.parts
    start = jnp.arange(plan.n_ctx)[:, None] * plan.span + section * plan.half + part * plan.sub
    return (start + jnp.arange(plan.sub)[None, :]).reshape(-1)


def rope_tables(positions):
    half_width = HD // 2
    frequency = jnp.power(10000.0, -(jnp.arange(half_width).astype(F32) * 2.0) / HD)
    angles = positions.astype(F32)[:, None] * frequency[None, :]
    cos, sin = jnp.cos(angles), jnp.sin(angles)
    return jnp.concatenate([cos] * 4, axis=1), jnp.concatenate([-sin, sin, -sin, sin], axis=1)


def local(tokens, upstream, lengths, w_qkv, w_out, w_in, w_back, gain_attn, gain_ffn):
    plan = Plan(tokens, w_in)
    width = plan.width
    layers = 2

    qkv_low, out_low = w_qkv[0].astype(BF16), w_out[0].astype(BF16)
    in_low, back_low = w_in[0].astype(BF16), w_back[0].astype(BF16)
    here, there = plan.section, 1 - plan.section

    def halves(which):
        return (
            take_half(plan, qkv_low[:, : 2 * width], which),
            jnp.where(which == 0, qkv_low[:, 2 * width :], out_low),
            take_half(plan, in_low, which),
            take_half(plan, back_low, which),
        )

    kept = halves(here)
    got = [other_core(value) for value in halves(there)]
    shards = [
        [by_section(plan, k, g) for k, g in zip(kept, got)],
        [by_section(plan, g, k) for k, g in zip(kept, got)],
    ]

    source = to_sequences(plan, tokens).astype(F32)
    gains = gather_gains(plan, gain_attn, gain_ffn)
    weights = []
    for layer in range(layers):
        qk, vo, first, second = shards[layer]
        weights.append(
            (
                spread(plan, qk, True),
                spread(plan, vo, False),
                spread(plan, first, True),
                spread(plan, second, False),
            )
        )
    cotangent = to_sequences(plan, upstream)

    cos, sin = rope_tables(positions_of(plan, plan.section, plan.ctx))
    sequence = plan.ctx // plan.parts
    length = lax.dynamic_index_in_dim(lengths.reshape(-1), sequence, 0, keepdims=False)
    places = []
    for mask in range(plan.parts):
        for core in range(2):
            places.append(positions_of(plan, plan.section ^ core, plan.ctx ^ mask))
    hidden_key = jnp.where(jnp.concatenate(places) < length, 0.0, MASKED)
    lane = jnp.arange(PAIR)
    bias = jnp.where(lane[None, :] == 0, hidden_key[:, None], 0.0).astype(BF16)

    saved, acts = [], []
    x = source
    for layer in range(layers):
        qk, vo, first, second = weights[layer]
        a, query, own_kv = qkv_forward(plan, x, gains[layer, 0], cos, sin, qk, vo)
        kv = shared_keys(plan, own_kv)
        o, lse = attention_forward(plan, query, kv, bias)
        u2, b = out_forward(plan, o, x, gains[layer, 1], vo)
        result, low, h, slope = ffn_forward(plan, b, u2, first, second)
        saved.append((x, a, query, kv, o, lse, u2, b, h, slope))
        acts.append(from_sequences(plan, low))
        x = result

    c = cotangent
    grads, sums, dgains = [None] * layers, [None] * layers, [None] * layers
    for layer in reversed(range(layers)):
        qk, vo, first, second = weights[layer]
        x, a, query, kv, o, lse, u2, b, h, slope = saved[layer]
        cf, dhp, du2, dz, do, dg2 = ffn_backward(
            plan, c, slope, u2, gains[layer, 1], first, second, vo
        )
        d_in = weight_grad(plan, b, dhp, plan.hidden // 2, 0, True)
        d_back = weight_grad(plan, h, cf, width // 2, 0, False)
        dq, dk, dv, *far = attention_backward(plan, query, do, o, lse, bias, kv)
        far = return_keys(plan, far)
        d_out = weight_grad(plan, o, dz, width // 2, 0, True)
        dqkv, dx, low, dg1 = qkv_backward(
            plan, dq, dk, dv, far, du2, x, gains[layer, 0], cos, sin, qk, vo
        )
        wide = 3 * width // 2
        cut = (wide // 2 + 127) // 128 * 128
        d_qkv = jnp.concatenate(
            [
                weight_grad(plan, a, dqkv, cut, 0, True),
                weight_grad(plan, a, dqkv, wide - cut, cut, False),
            ],
            axis=1,
        )
        grads[layer] = from_sequences(plan, low)
        sums[layer] = (d_qkv, d_out, d_in, d_back)
        dgains[layer] = (dg1, dg2)
        c = dx

    def to_owner(first, second):
        own = by_section(plan, first, second)
        got = other_core(by_section(plan, second, first))
        left, right = by_section(plan, own, got), by_section(plan, got, own)
        return jnp.concatenate([left, right], axis=1).astype(F32)[None]

    weight_grads = [to_owner(one, two) for one, two in zip(*sums)]
    gain_sums = sum_gains(plan, jnp.concatenate([g for pair in dgains for g in pair], axis=0))
    return (to_output(plan, acts), to_output(plan, grads), *weight_grads, *gain_sums)


def solution(mesh):
    rows = P(None, "dp", "ctx", None)
    weight = P("section", ("dp", "ctx"), None)
    gain = P("section", ("dp", "ctx"))
    out_rows = P("section", None, "dp", "ctx", None)
    return jax.shard_map(
        local,
        mesh=mesh,
        in_specs=(rows, rows, P(None, "dp"), weight, weight, weight, weight, gain, gain),
        out_specs=(out_rows, out_rows, weight, weight, weight, weight, gain, gain),
        check_vma=False,
    )
```

```python
import functools

import jax
import jax.numpy as jnp
from jax import lax
from jax.experimental import pallas as pl
from jax.experimental.pallas import tpu as pltpu
from jax.sharding import PartitionSpec as P

HD = 64
PAIR = 2 * HD
BF16 = jnp.bfloat16
F32 = jnp.float32
MASKED = -1e30
COST_SHARE = 0.1
GAIN_LANES = 128


def nn(left, right):
    return lax.dot_general(left, right, (((1,), (0,)), ((), ())), preferred_element_type=F32)


def nt(left, right):
    return lax.dot_general(left, right, (((1,), (1,)), ((), ())), preferred_element_type=F32)


def tn(left, right):
    return lax.dot_general(left, right, (((0,), (0,)), ((), ())), preferred_element_type=F32)


def normalise(rows):
    centred = rows - jnp.mean(rows, axis=-1, keepdims=True)
    scale = lax.rsqrt(jnp.mean(centred * centred, axis=-1, keepdims=True) + 1e-05)
    return centred * scale, scale


def norm_back(rows, gain, grad):
    normed, scale = normalise(rows)
    inner = grad * gain
    mean_inner = jnp.mean(inner, axis=-1, keepdims=True)
    mean_along = jnp.mean(inner * normed, axis=-1, keepdims=True)
    grad_rows = scale * (inner - mean_inner - normed * mean_along)
    return grad_rows, jnp.sum(grad * normed, axis=0, keepdims=True)


def swap_halves(pair_block):
    lane = lax.broadcasted_iota(jnp.int32, pair_block.shape, 1)
    ahead = pltpu.roll(pair_block, PAIR - HD // 2, 1)
    behind = pltpu.roll(pair_block, HD // 2, 1)
    return jnp.where(lane % HD < HD // 2, ahead, behind)


class Plan:
    def __init__(self, tokens, w_in):
        micro, seqs, span, width = tokens.shape
        self.width = width
        self.hidden = w_in.shape[-1]
        self.heads = width // HD
        self.pairs = width // PAIR
        self.n_ctx = lax.axis_size("ctx")
        self.n_dp = lax.axis_size("dp")
        self.micro, self.seqs, self.span = micro, seqs, span
        self.n_seq = micro * seqs
        self.parts = self.n_ctx // self.n_seq
        assert self.parts * self.n_seq == self.n_ctx
        self.half = span // 2
        self.sub = self.half // self.parts
        self.rows = self.n_ctx * self.sub
        self.section = lax.axis_index("section")
        self.dp = lax.axis_index("dp")
        self.ctx = lax.axis_index("ctx")
        self.staged = w_in.shape[1] % 16 == 0 and self.n_ctx == 4 and self.n_dp == 4
        self.blocks = self.n_dp if self.staged else 1
        self.shards = self.n_dp * self.n_ctx if self.staged else 1
        self.shard_rows = width // self.shards
        self.meta = jnp.stack([self.section, self.dp]).astype(jnp.int32)


X_BIT, Y_BIT = 1, 2


def other_core(value):
    return lax.ppermute(value, "section", [(0, 1), (1, 0)])


def xor_dp(plan, value, mask):
    return lax.ppermute(value, "dp", [(i, i ^ mask) for i in range(plan.n_dp)])


def xor_ctx(plan, value, mask):
    return lax.ppermute(value, "ctx", [(i, i ^ mask) for i in range(plan.n_ctx)])


def exchange_ctx(value, dim=0):
    return lax.all_to_all(value, "ctx", dim, dim, tiled=True)


def spread_ctx(plan, shard):
    return exchange_ctx(jnp.concatenate([shard] * plan.n_ctx, axis=0))


def after(value, *earlier):
    earlier = [item for item in earlier if item is not None]
    if not earlier:
        return value
    return lax.optimization_barrier((value, *earlier))[0]


class Spread:
    def __init__(self, own, relative):
        self.own, self.relative = own, relative

    def share(self, *earlier):
        self.other = other_core(after(self.own, *earlier))

    def refs(self):
        return [self.own, self.other]


def to_lanes_of_halves(tall):
    half = tall.shape[1] // 2
    return jnp.concatenate([to_lanes(tall[:, :half]), to_lanes(tall[:, half:])], axis=1)


def to_lanes(tall):
    rows = tall.shape[0] // 4
    return jnp.concatenate([tall[i * rows : (i + 1) * rows] for i in range(4)], axis=1)


def from_lanes(wide):
    cols = wide.shape[1] // 4
    return jnp.concatenate([wide[:, i * cols : (i + 1) * cols] for i in range(4)], axis=0)


def gather_natural(plan, shard, tall=0):
    gathered = lax.all_gather(shard, ("dp", "ctx"), axis=0, tiled=True)
    if plan.staged:
        return Spread(gathered.reshape(plan.shards, plan.shard_rows, -1), False)
    if tall:
        cut = gathered.shape[1] - tall
        n = plan.n_dp * plan.n_ctx
        quarters = gathered[:, cut:].reshape(n, plan.width // n, 4, tall // 4).transpose(0, 2, 1, 3)
        gathered = jnp.concatenate([gathered[:, :cut], to_lanes(quarters.reshape(-1, tall // 4))], axis=1)
    return Spread(gathered[None], False)


class SpreadDp:
    def __init__(self, plan, block, *earlier):
        self.plan = plan
        self.block = after(block, *earlier)
        self.got = [xor_dp(plan, self.block, mask) for mask in (X_BIT, Y_BIT, X_BIT | Y_BIT)]

    def result(self, *earlier):
        plan = self.plan
        blocks = jnp.stack([after(self.block, *earlier), *self.got])
        return Spread(blocks.reshape(plan.shards, plan.shard_rows, -1), True)


class Collect:
    def __init__(self, plan, blocks):
        self.plan = plan
        self.blocks = [blocks[0]] + [xor_dp(plan, blocks[mask], mask) for mask in range(1, plan.n_dp)]

    def first(self, order):
        order.need(*self.blocks[1:])

    def second(self, order):
        plan = self.plan
        own = order.gate(self.blocks[0])
        block = sum(value.astype(F32) for value in [own, *self.blocks[1:]]).astype(BF16)
        order.mark(block)
        self.parts = exchange_ctx(block.reshape(plan.n_ctx, plan.shard_rows, -1))

    def last(self, order):
        order.need(self.parts)

    def result(self):
        return jnp.sum(self.parts.astype(F32), axis=0).astype(BF16)


def smem():
    return pl.BlockSpec(memory_space=pltpu.SMEM)


def anywhere():
    return pl.BlockSpec(memory_space=pl.ANY)


def whole(shape):
    return pl.BlockSpec(shape, lambda i: (0,) * len(shape))


def rows_of(step, width):
    return pl.BlockSpec((step, width), lambda i: (i, 0))


def params(megabytes):
    return pltpu.CompilerParams(vmem_limit_bytes=megabytes * 1024 * 1024)


def cost(flops, bytes_accessed, transcendentals=0):
    return pl.CostEstimate(
        flops=int(flops * COST_SHARE),
        bytes_accessed=int(bytes_accessed * COST_SHARE),
        transcendentals=int(transcendentals * COST_SHARE),
    )


def block_copies(meta, ref, relative, place, lanes, sems, first):
    blocks = 4 if relative else 1
    count = ref.shape[0] // blocks
    copies = []
    for mask in range(blocks):
        start = (meta[1] ^ mask) * count if relative else 0
        copies.append(
            pltpu.make_async_copy(
                ref.at[pl.ds(mask * count, count), :, lanes],
                place(pl.ds(start, count)),
                sems.at[first + mask],
            )
        )
    return copies


def run(copies):
    for copy in copies:
        copy.start()


def wait(copies):
    for copy in copies:
        copy.wait()


class Loads:
    def __init__(self, section, own, other, carrier=None):
        self.section, self.own, self.other, self.carrier = section, own, other, carrier

    def each(self, act):
        if self.carrier is None:
            act(self.own)
            act(self.other)
            return
        pl.when(self.section == self.carrier)(lambda: act(self.own))
        pl.when(self.section != self.carrier)(lambda: act(self.other))

    def start(self):
        self.each(run)

    def wait(self):
        self.each(wait)


def split_refs(refs, counts):
    out, at = [], 0
    for count in counts:
        out.append(refs[at : at + count])
        at += count
    return out


def side(which, half):
    return pl.ds(pl.multiple_of(which * half, 128), half)


def load_halves(meta, relative, refs, matrix, start, sems, first):
    half = matrix.shape[-1] // 2
    lanes = slice(start, start + half)

    def at(which):
        return lambda shards: matrix.at[shards, :, side(which, half)]

    own = block_copies(meta, refs[0], relative, at(meta[0]), lanes, sems, first)
    other = block_copies(meta, refs[1], relative, at(1 - meta[0]), lanes, sems, first + 4)
    return Loads(meta[0], own, other)


def load_tall(meta, relative, refs, matrix, start, sems, first):
    half = matrix.shape[-1] // 2
    own, other = [], []
    for quarter in range(4):
        lanes = slice(start + quarter * half, start + (quarter + 1) * half)

        def at(which, quarter=quarter):
            return lambda shards: matrix.at[shards, quarter, :, side(which, half)]

        where = first + 8 * quarter
        own += block_copies(meta, refs[0], relative, at(meta[0]), lanes, sems, where)
        other += block_copies(meta, refs[1], relative, at(1 - meta[0]), lanes, sems, where + 4)
    return Loads(meta[0], own, other)


def load_one(meta, relative, refs, matrix, start, sems, first, carrier):
    lanes = slice(start, start + matrix.shape[-1])

    def at(shards):
        return matrix.at[shards]

    own = block_copies(meta, refs[0], relative, at, lanes, sems, first)
    other = block_copies(meta, refs[1], relative, at, lanes, sems, first)
    return Loads(meta[0], own, other, carrier)


def flat(matrix):
    return matrix.reshape(-1, matrix.shape[-1])


def row_step(rows, step=128):
    return step if rows % step == 0 else rows


def qkv_kernel(relative, meta, x_ref, cos_ref, sin_ref, *refs):
    attn_refs, rest = split_refs(refs, (2, len(refs) - 2))
    a_ref, q_ref, kv_ref, gains_ref, wqk, wv, columns, sems = rest
    width = wv.shape[-1]
    qk = load_halves(meta, relative, attn_refs, wqk, 0, sems, 0)
    v = load_one(meta, relative, attn_refs, wv, width, sems, 8, 0)
    gain = load_one(meta, relative, attn_refs, columns, 2 * width, sems, 12, 0)
    first = pl.program_id(0) == 0

    @pl.when(first)
    def _():
        gain.start()
        qk.start()
        v.start()
        gain.wait()
        gains_ref[...] = jnp.transpose(flat(columns[...]).astype(F32))[:8]

    normed, _ = normalise(x_ref[...].astype(F32))
    a = (normed * gains_ref[0:1, :]).astype(BF16)
    a_ref[...] = jnp.transpose(a)

    @pl.when(first)
    def _():
        qk.wait()
        v.wait()

    cos, sin = cos_ref[...], sin_ref[...]
    for which in range(2):
        out = nn(a, flat(wqk[:, :, which * width : (which + 1) * width]))
        for pair in range(width // PAIR):
            lanes = slice(pair * PAIR, (pair + 1) * PAIR)
            block = out[:, lanes]
            turned = block * cos + swap_halves(block) * sin
            if which == 0:
                q_ref[:, lanes] = (turned * HD**-0.5).astype(BF16)
            else:
                kv_ref[0, :, lanes] = turned.astype(BF16)
    kv_ref[1] = nn(a, flat(wv[...])).astype(BF16)


def qkv_forward(plan, x, cos, sin, attn):
    rows, width = x.shape
    step = row_step(rows)
    return pl.pallas_call(
        functools.partial(qkv_kernel, attn.relative),
        out_shape=[
            jax.ShapeDtypeStruct((width, rows), BF16),
            jax.ShapeDtypeStruct((rows, width), BF16),
            jax.ShapeDtypeStruct((2, rows, width), BF16),
            jax.ShapeDtypeStruct((8, width), F32),
        ],
        grid=(rows // step,),
        in_specs=[smem(), rows_of(step, width), rows_of(step, PAIR), rows_of(step, PAIR)]
        + [anywhere()] * 2,
        out_specs=[
            pl.BlockSpec((width, step), lambda i: (0, i)),
            rows_of(step, width),
            pl.BlockSpec((2, step, width), lambda i: (0, i, 0)),
            whole((8, width)),
        ],
        scratch_shapes=[
            pltpu.VMEM((plan.shards, plan.shard_rows, 2 * width), BF16),
            pltpu.VMEM((plan.shards, plan.shard_rows, width), BF16),
            pltpu.VMEM((plan.shards, plan.shard_rows, GAIN_LANES), BF16),
            pltpu.SemaphoreType.DMA((16,)),
        ],
        compiler_params=params(56),
        cost_estimate=cost(6 * rows * width * width, 12 * rows * width + 6 * width * width),
        name="qkv_forward",
    )(plan.meta, x, cos, sin, *attn.refs())


def lane_mask(shape, head):
    lane = lax.broadcasted_iota(jnp.int32, shape, 1)
    return lane < HD if head == 0 else lane >= HD


def with_ones(query):
    lane = lax.broadcasted_iota(jnp.int32, query.shape, 1)
    return jnp.concatenate([query, jnp.where(lane == 0, 1.0, 0.0).astype(BF16)], axis=1)


def attention_kernel(chunks, key_block, q_ref, *refs):
    kv = refs[:chunks]
    bias_ref, o_ref, ot_ref, lse_ref, s_scr, vt_scr = refs[chunks:]
    rows = q_ref.shape[0]
    per_chunk = rows // key_block
    query = q_ref[...]
    for c in range(chunks):
        vt_scr[:, c * rows : (c + 1) * rows] = jnp.transpose(kv[c][1])
    outs = []
    for head in range(2):
        extended = with_ones(jnp.where(lane_mask(query.shape, head), query, jnp.zeros_like(query)))
        peak = jnp.full((1, rows), -jnp.inf, F32)
        for c in range(chunks):
            for j in range(per_chunk):
                at = slice(j * key_block, (j + 1) * key_block)
                everywhere = slice(c * rows + at.start, c * rows + at.stop)
                keys = jnp.concatenate([kv[c][0, at, :], bias_ref[everywhere, :]], axis=1)
                scores = nt(keys, extended)
                s_scr[everywhere, :] = scores
                peak = jnp.maximum(peak, jnp.max(scores, axis=0, keepdims=True))
        total = jnp.zeros((1, rows), F32)
        out = jnp.zeros((PAIR, rows), F32)
        for c in range(chunks):
            for j in range(per_chunk):
                everywhere = slice(c * rows + j * key_block, c * rows + (j + 1) * key_block)
                weights = jnp.exp(s_scr[everywhere, :] - peak)
                total = total + jnp.sum(weights, axis=0, keepdims=True)
                out = out + nn(vt_scr[:, everywhere], weights.astype(BF16))
        lse_ref[0, head : head + 1, :] = peak + jnp.log(total)
        outs.append(out / total)
    row = lax.broadcasted_iota(jnp.int32, outs[0].shape, 0)
    out = jnp.where(row < HD, outs[0], outs[1])
    o_ref[...] = jnp.transpose(out).astype(BF16)
    ot_ref[...] = out.astype(BF16)


def attention_forward(plan, query, kv, bias):
    rows, width = query.shape
    chunks = len(kv)
    keys = chunks * rows
    pair_block = pl.BlockSpec((rows, PAIR), lambda p: (0, p))
    kv_block = pl.BlockSpec((2, rows, PAIR), lambda p: (0, 0, p))
    return pl.pallas_call(
        functools.partial(attention_kernel, chunks, min(256, rows)),
        out_shape=[
            jax.ShapeDtypeStruct((rows, width), BF16),
            jax.ShapeDtypeStruct((width, rows), BF16),
            jax.ShapeDtypeStruct((plan.pairs, 8, rows), F32),
        ],
        grid=(plan.pairs,),
        in_specs=[pair_block] + [kv_block] * chunks + [pl.BlockSpec((keys, PAIR), lambda p: (0, 0))],
        out_specs=[
            pair_block,
            pl.BlockSpec((PAIR, rows), lambda p: (p, 0)),
            pl.BlockSpec((1, 8, rows), lambda p: (p, 0, 0)),
        ],
        scratch_shapes=[pltpu.VMEM((keys, rows), F32), pltpu.VMEM((PAIR, keys), BF16)],
        compiler_params=params(56),
        cost_estimate=cost(
            16 * rows * keys * width, 4 * rows * width + 4 * keys * width, rows * keys * plan.heads
        ),
        name="attention_forward",
    )(query, *kv, bias)


def layer_loads(meta, relative, attn_refs, ffn_refs, wo, w1, w2, sems):
    half = w1.shape[-1] // 2
    out = load_one(meta, relative[0], attn_refs, wo, wo.shape[-1], sems, 0, 1)
    first = load_halves(meta, relative[1], ffn_refs, w1, 0, sems, 4)
    second = load_tall(meta, relative[1], ffn_refs, w2, half, sems, 12)
    return out, first, second


def layer_scratch(plan):
    width, hidden, n, rows = plan.width, plan.hidden, plan.shards, plan.shard_rows
    return [
        pltpu.VMEM((n, rows, width), BF16),
        pltpu.VMEM((n, rows, hidden), BF16),
        pltpu.VMEM((n, 4, rows, width), BF16),
        pltpu.SemaphoreType.DMA((44,)),
    ]


def tall_chunk(w2, i):
    n = w2.shape[0]
    value = w2[pl.ds(i * (n // 4), n // 4)] if n >= 4 else w2[0, i]
    return flat(value)


def ffn_kernel(relative, meta, o_ref, x_ref, gains_ref, *refs):
    attn_refs, ffn_refs, rest = split_refs(refs, (2, 2, len(refs) - 4))
    u2_ref, bt_ref, acts_ref, low_ref, ht_ref, slope_ref, wo, w1, w2, sems, b_ref = rest
    out, first, second = layer_loads(meta, relative, attn_refs, ffn_refs, wo, w1, w2, sems)
    chunk = slope_ref.shape[1]
    i = pl.program_id(0)

    @pl.when(i == 0)
    def _():
        out.start()
        first.start()
        second.start()
        out.wait()
        u2 = x_ref[...].astype(F32) + nn(o_ref[...], flat(wo[...]))
        u2_ref[...] = u2
        acts_ref[...] = u2
        b = (normalise(u2)[0] * gains_ref[1:2, :]).astype(BF16)
        b_ref[...] = b
        bt_ref[...] = jnp.transpose(b)
        first.wait()
        second.wait()

    at = pl.ds(pl.multiple_of(i * chunk, chunk), chunk)
    hp = nn(b_ref[...], flat(w1[:, :, at]))
    cdf = 0.5 * (1.0 + lax.erf(hp * (0.5**0.5)))
    density = jnp.exp(-0.5 * hp * hp) * 0.3989422804014327
    h = (hp * cdf).astype(BF16)
    ht_ref[...] = jnp.transpose(h)
    slope_ref[...] = (cdf + hp * density).astype(BF16)
    acts_ref[...] += nn(h, tall_chunk(w2, i))

    @pl.when(i == pl.num_programs(0) - 1)
    def _():
        low_ref[...] = acts_ref[...].astype(BF16)


def ffn_forward(plan, o, x, gains, attn, ffn):
    rows, width = x.shape
    hidden = plan.hidden
    chunk = hidden // 4
    refs = [*attn.refs(), *ffn.refs()]
    relative = (attn.relative, ffn.relative)
    columns = pl.BlockSpec((rows, chunk), lambda i: (0, i))
    return pl.pallas_call(
        functools.partial(ffn_kernel, relative),
        out_shape=[
            jax.ShapeDtypeStruct((rows, width), F32),
            jax.ShapeDtypeStruct((width, rows), BF16),
            jax.ShapeDtypeStruct((rows, width), F32),
            jax.ShapeDtypeStruct((rows, width), BF16),
            jax.ShapeDtypeStruct((hidden, rows), BF16),
            jax.ShapeDtypeStruct((rows, hidden), BF16),
        ],
        grid=(hidden // chunk,),
        in_specs=[smem(), whole((rows, width)), whole((rows, width)), whole((8, width))]
        + [anywhere()] * len(refs),
        out_specs=[whole((rows, width)), whole((width, rows)), whole((rows, width)), whole((rows, width))]
        + [rows_of(chunk, rows), columns],
        scratch_shapes=[
            *layer_scratch(plan),
            pltpu.VMEM((rows, width), BF16),
        ],
        compiler_params=params(56),
        cost_estimate=cost(
            4 * rows * width * hidden + 2 * rows * width * width + 60 * rows * hidden,
            20 * rows * width + 4 * rows * hidden + 4 * width * hidden,
            2 * rows * hidden,
        ),
        name="ffn_forward",
    )(plan.meta, o, x, gains, *refs)


def ffn_back_kernel(relative, meta, c_ref, slope_ref, u2_ref, gains_ref, *refs):
    attn_refs, ffn_refs, rest = split_refs(refs, (2, 2, len(refs) - 4))
    cf_ref, dhp_ref, du2_ref, dz_ref, do_ref, dg_ref, wo, w1, w2, sems, acc = rest
    out, first, second = layer_loads(meta, relative, attn_refs, ffn_refs, wo, w1, w2, sems)
    chunk = dhp_ref.shape[1]
    i = pl.program_id(0)

    @pl.when(i == 0)
    def _():
        second.start()
        first.start()
        out.start()
        cf_ref[...] = c_ref[...].astype(BF16)
        acc[...] = jnp.zeros_like(acc)
        second.wait()
        first.wait()
        out.wait()

    at = pl.ds(pl.multiple_of(i * chunk, chunk), chunk)
    dh = nt(cf_ref[...], tall_chunk(w2, i))
    dhp = (dh * slope_ref[...].astype(F32)).astype(BF16)
    dhp_ref[...] = dhp
    acc[...] += nt(dhp, flat(w1[:, :, at]))

    @pl.when(i == pl.num_programs(0) - 1)
    def _():
        grad, dgain = norm_back(u2_ref[...], gains_ref[1:2, :], acc[...])
        du2 = c_ref[...].astype(F32) + grad
        du2_ref[...] = du2
        dg_ref[...] = dgain
        dz = du2.astype(BF16)
        dz_ref[...] = dz
        do_ref[...] = nt(dz, flat(wo[...])).astype(BF16)


def ffn_backward(plan, c, slope, u2, gains, attn, ffn):
    rows, width = u2.shape
    hidden = plan.hidden
    chunk = hidden // 4
    refs = [*attn.refs(), *ffn.refs()]
    relative = (attn.relative, ffn.relative)
    columns = pl.BlockSpec((rows, chunk), lambda i: (0, i))
    wide = jax.ShapeDtypeStruct((rows, width), BF16)
    full = whole((rows, width))
    return pl.pallas_call(
        functools.partial(ffn_back_kernel, relative),
        out_shape=[
            wide,
            jax.ShapeDtypeStruct((rows, hidden), BF16),
            jax.ShapeDtypeStruct((rows, width), F32),
            wide,
            wide,
            jax.ShapeDtypeStruct((1, width), F32),
        ],
        grid=(hidden // chunk,),
        in_specs=[smem(), full, columns, full, whole((8, width))] + [anywhere()] * len(refs),
        out_specs=[full, columns, full, full, full, whole((1, width))],
        scratch_shapes=[
            *layer_scratch(plan),
            pltpu.VMEM((rows, width), F32),
        ],
        compiler_params=params(56),
        cost_estimate=cost(
            4 * rows * width * hidden + 2 * rows * width * width,
            18 * rows * width + 4 * rows * hidden + 4 * width * hidden + 2 * width * width,
        ),
        name="ffn_backward",
    )(plan.meta, c, slope, u2, gains, *refs)


def attention_back_kernel(chunks, key_block, q_ref, do_ref, o_ref, lse_ref, bias_ref, *refs):
    kv = refs[:chunks]
    dq_ref, dk_ref, dv_ref = refs[chunks : chunks + 3]
    far = refs[chunks + 3 : 2 * chunks + 2]
    kt_scr, dk_scr, dv_scr = refs[2 * chunks + 2 :]
    rows = q_ref.shape[0]
    per_chunk = rows // key_block
    query, grad = q_ref[...], do_ref[...]
    for c in range(chunks):
        kt_scr[:, c * rows : (c + 1) * rows] = jnp.transpose(kv[c][0])
    products = jnp.transpose(grad.astype(F32) * o_ref[...].astype(F32))
    outs = []
    for head in range(2):
        mask = lane_mask(query.shape, head)
        masked_query = jnp.where(mask, query, jnp.zeros_like(query))
        masked_grad = jnp.where(mask, grad, jnp.zeros_like(grad))
        extended = with_ones(masked_query)
        delta = jnp.sum(products[head * HD : (head + 1) * HD], axis=0, keepdims=True)
        lse = lse_ref[0, head : head + 1, :]
        dqt = jnp.zeros((PAIR, rows), F32)
        for c in range(chunks):
            for j in range(per_chunk):
                at = slice(j * key_block, (j + 1) * key_block)
                everywhere = slice(c * rows + at.start, c * rows + at.stop)
                keys = jnp.concatenate([kv[c][0, at, :], bias_ref[everywhere, :]], axis=1)
                weights = jnp.exp(nt(keys, extended) - lse)
                grad_weights = nt(kv[c][1, at, :], masked_grad)
                grad_scores = (weights * (grad_weights - delta)).astype(BF16)
                dv = nn(weights.astype(BF16), masked_grad)
                dk = nn(grad_scores, masked_query)
                dqt = dqt + nn(kt_scr[:, everywhere], grad_scores)
                if head == 0:
                    dv_scr[everywhere, :] = dv
                    dk_scr[everywhere, :] = dk
                elif c == 0:
                    dk_ref[at, :] = dk_scr[everywhere, :] + dk
                    dv_ref[at, :] = dv_scr[everywhere, :] + dv
                else:
                    far[c - 1][0, at, :] = (dk_scr[everywhere, :] + dk).astype(BF16)
                    far[c - 1][1, at, :] = (dv_scr[everywhere, :] + dv).astype(BF16)
        outs.append(dqt)
    row = lax.broadcasted_iota(jnp.int32, outs[0].shape, 0)
    dq_ref[...] = jnp.transpose(jnp.where(row < HD, outs[0], outs[1])).astype(BF16)


def attention_backward(plan, query, grad, o, lse, bias, kv):
    rows, width = query.shape
    chunks = len(kv)
    keys = chunks * rows
    pair_block = pl.BlockSpec((rows, PAIR), lambda p: (0, p))
    kv_block = pl.BlockSpec((2, rows, PAIR), lambda p: (0, 0, p))
    near = jax.ShapeDtypeStruct((rows, width), F32)
    return pl.pallas_call(
        functools.partial(attention_back_kernel, chunks, min(256, rows)),
        out_shape=[jax.ShapeDtypeStruct((rows, width), BF16), near, near]
        + [jax.ShapeDtypeStruct((2, rows, width), BF16)] * (chunks - 1),
        grid=(plan.pairs,),
        in_specs=[pair_block] * 3
        + [
            pl.BlockSpec((1, 8, rows), lambda p: (p, 0, 0)),
            pl.BlockSpec((keys, PAIR), lambda p: (0, 0)),
        ]
        + [kv_block] * chunks,
        out_specs=[pair_block] * 3 + [kv_block] * (chunks - 1),
        scratch_shapes=[
            pltpu.VMEM((PAIR, keys), BF16),
            pltpu.VMEM((keys, PAIR), F32),
            pltpu.VMEM((keys, PAIR), F32),
        ],
        compiler_params=params(56),
        cost_estimate=cost(
            40 * rows * keys * width,
            16 * rows * width + 8 * keys * width,
            rows * keys * plan.heads,
        ),
        name="attention_backward",
    )(query, grad, o, lse, bias, *kv)


def qkv_back_kernel(
    spread, n_far, meta, dq_ref, dk_ref, dv_ref, du2_ref, x_ref, gains_ref, cos_ref, sin_ref, *refs
):
    far, attn_refs, rest = split_refs(refs, (n_far, len(refs) - n_far - 7, 7))
    dqkv_ref, dx_ref, low_ref, dg_ref, wqk, wv, sems = rest
    qk = load_halves(meta, spread, attn_refs, wqk, 0, sems, 0)
    v = load_one(meta, spread, attn_refs, wv, wv.shape[-1], sems, 8, 0)
    first = pl.program_id(0) == 0

    @pl.when(first)
    def _():
        qk.start()
        v.start()
        dg_ref[...] = jnp.zeros_like(dg_ref)

    width = x_ref.shape[1]
    cos, sin = cos_ref[...], sin_ref[...]
    for pair in range(width // PAIR):
        lanes = slice(pair * PAIR, (pair + 1) * PAIR)
        dq = dq_ref[:, lanes].astype(F32) * HD**-0.5
        dk, dv = dk_ref[:, lanes], dv_ref[:, lanes]
        for part in far:
            dk = dk + part[0, :, lanes].astype(F32)
            dv = dv + part[1, :, lanes].astype(F32)
        dk = dk.astype(BF16).astype(F32)
        dqkv_ref[:, pair * PAIR : (pair + 1) * PAIR] = (dq * cos - swap_halves(dq) * sin).astype(BF16)
        at = width + pair * PAIR
        dqkv_ref[:, at : at + PAIR] = (dk * cos - swap_halves(dk) * sin).astype(BF16)
        at = 2 * width + pair * PAIR
        dqkv_ref[:, at : at + PAIR] = dv.astype(BF16)

    @pl.when(first)
    def _():
        qk.wait()
        v.wait()

    da = nt(dqkv_ref[:, : 2 * width], flat(wqk[...]))
    da = da + nt(dqkv_ref[:, 2 * width :], flat(wv[...]))
    grad, dgain = norm_back(x_ref[...].astype(F32), gains_ref[0:1, :], da)
    dx = du2_ref[...] + grad
    dx_ref[...] = dx
    low_ref[...] = dx.astype(BF16)
    dg_ref[...] += dgain


def qkv_backward(plan, dq, dk, dv, far, du2, x, gains, cos, sin, attn):
    rows, width = x.shape
    step = row_step(rows)
    refs = attn.refs()
    some = rows_of(step, width)
    return pl.pallas_call(
        functools.partial(qkv_back_kernel, attn.relative, len(far)),
        out_shape=[
            jax.ShapeDtypeStruct((rows, 3 * width), BF16),
            jax.ShapeDtypeStruct((rows, width), F32),
            jax.ShapeDtypeStruct((rows, width), BF16),
            jax.ShapeDtypeStruct((1, width), F32),
        ],
        grid=(rows // step,),
        in_specs=[smem()]
        + [some] * 5
        + [whole((8, width)), rows_of(step, PAIR), rows_of(step, PAIR)]
        + [pl.BlockSpec((2, step, width), lambda i: (0, i, 0))] * len(far)
        + [anywhere()] * len(refs),
        out_specs=[rows_of(step, 3 * width), some, some, whole((1, width))],
        scratch_shapes=[
            pltpu.VMEM((plan.shards, plan.shard_rows, 2 * width), BF16),
            pltpu.VMEM((plan.shards, plan.shard_rows, width), BF16),
            pltpu.SemaphoreType.DMA((12,)),
        ],
        compiler_params=params(56),
        cost_estimate=cost(6 * rows * width * width, 30 * rows * width + 6 * width * width),
        name="qkv_backward",
    )(plan.meta, dq, dk, dv, du2, x, gains, cos, sin, *far, *refs)


class Job:
    def __init__(self, left, right, start, cols, tall=False):
        self.left, self.right, self.start, self.cols, self.tall = left, right, start, cols, tall
        self.lanes = 4 * cols if tall else cols
        self.given = right is None


def weight_kernel(jobs, n_lefts, n_rights, mine, relative, meta, *refs):
    n_got = 1 if mine else 0
    lefts, rights, got, outs, (acc,) = split_refs(
        refs, (n_lefts, n_rights, n_got, len(refs) - n_lefts - n_rights - n_got - 1, 1)
    )
    step = pl.program_id(0)
    which = meta[0] if mine else 1 - meta[0]
    block = (meta[1] ^ step) if relative else step

    shards, size = acc.shape[:2]
    lane = 0
    for job in jobs:
        left = lefts[job.left]
        if job.given:
            count = shards * size
            rows = left[pl.ds(pl.multiple_of(block * count, 16), count), :]
            acc[:, :, lane : lane + job.cols] = rows.reshape(shards, size, job.cols)
            lane += job.cols
            continue
        right = rights[job.right]
        half = right.shape[1] // 2
        columns = right[:, side(which, half)] if job.cols == half else right[
            :, pl.ds(pl.multiple_of(which * half + job.start, 128), job.cols)
        ]
        count = shards * size * (4 if job.tall else 1)
        product = nn(left[pl.ds(pl.multiple_of(block * count, 16), count), :], columns)
        if job.tall:
            product = product.reshape(shards, 4, size, job.cols)
            for quarter in range(4):
                acc[:, :, lane : lane + job.cols] = product[:, quarter]
                lane += job.cols
        else:
            acc[:, :, lane : lane + job.cols] = product.reshape(shards, size, job.cols)
            lane += job.cols
    if not mine:
        outs[0][0] = acc[...].astype(BF16)
    elif len(outs) == 1:
        outs[0][0] = (acc[...] + got[0][0].astype(F32)).astype(BF16)
    else:
        for mask, out in enumerate(outs):

            @pl.when(step == mask)
            def _(out=out):
                out[...] = (acc[...] + got[0][0].astype(F32)).astype(BF16)


def weight_call(plan, lefts, rights, jobs, got, relative):
    rows = lefts[0].shape[1]
    n = plan.blocks
    mine = got is not None
    shape = (plan.shards // n, plan.shard_rows, sum(job.lanes for job in jobs))
    block = pl.BlockSpec((1, *shape), lambda i: (i, 0, 0, 0))
    if mine and relative:
        out_shape = [jax.ShapeDtypeStruct(shape, BF16)] * n
        out_specs = [whole(shape)] * n
    else:
        out_shape = [jax.ShapeDtypeStruct((n, *shape), BF16)]
        out_specs = [block]
    flops = sum(2 * rows * lefts[job.left].shape[0] * job.cols for job in jobs if not job.given)
    moved = sum(value.size * 2 for value in [*lefts, *rights])
    moved += 2 * n * shape[0] * shape[1] * shape[2] * (2 if mine else 1)
    result = pl.pallas_call(
        functools.partial(weight_kernel, jobs, len(lefts), len(rights), mine, relative),
        out_shape=out_shape,
        grid=(n,),
        in_specs=[smem()]
        + [whole(value.shape) for value in [*lefts, *rights]]
        + ([block] if mine else []),
        out_specs=out_specs,
        scratch_shapes=[pltpu.VMEM(shape, F32)],
        compiler_params=params(56),
        cost_estimate=cost(flops, moved),
        name="weight_mine" if mine else "weight_theirs",
    )(plan.meta, *lefts, *rights, *([got] if mine else []))
    return result if mine and relative else result[0]


class WeightGrads:
    def __init__(self, plan, lefts, rights, jobs, relative):
        self.plan, self.lefts, self.rights, self.jobs = plan, lefts, rights, jobs
        self.relative = relative and plan.staged

    def theirs(self, order):
        lefts = [order.gate(self.lefts[0]), *self.lefts[1:]]
        out = weight_call(self.plan, lefts, self.rights, self.jobs, None, self.relative)
        order.mark(out)
        self.got = other_core(out)

    def mine(self, order):
        plan = self.plan
        lefts = [order.gate(self.lefts[0]), *self.lefts[1:]]
        out = weight_call(plan, lefts, self.rights, self.jobs, self.got, self.relative)
        if self.relative:
            order.mark(out[0])
            self.sums = Collect(plan, out)
            return
        order.mark(out)
        tall = sum(job.lanes for job in self.jobs if job.tall)
        out = out.reshape(plan.width, -1)
        if plan.staged:
            self.total = lax.psum_scatter(out, ("dp", "ctx"), scatter_dimension=0, tiled=True)
            return
        cut = out.shape[1] - tall
        self.total = lax.psum_scatter(out[:, :cut], ("dp", "ctx"), scatter_dimension=0, tiled=True)
        if tall:
            part = from_lanes(out[:, cut:])
            part = lax.psum_scatter(part, ("dp", "ctx"), scatter_dimension=0, tiled=True)
            self.total = jnp.concatenate([self.total, to_lanes(part)], axis=1)

    def step(self, name, order):
        if self.relative:
            getattr(self.sums, name)(order)

    def result(self):
        return self.sums.result() if self.relative else self.total


class Order:
    def __init__(self):
        self.earlier = []

    def gate(self, value):
        return after(value, *self.earlier)

    def mark(self, value):
        self.earlier = [] if value is None else [value]

    def need(self, *values):
        self.earlier += [value for value in values if value is not None]


def by_section(plan, first, second):
    return jnp.where(plan.section == 0, first, second)


def take_half(plan, matrix, which):
    half = matrix.shape[-1] // 2
    return lax.dynamic_slice_in_dim(matrix, which * half, half, axis=matrix.ndim - 1)


def to_sequences(plan, tokens):
    pieces = tokens.reshape(plan.n_seq, 2, plan.half, plan.width)
    mine = lax.dynamic_index_in_dim(pieces, plan.section, 1, keepdims=False)
    mine = mine.reshape(plan.n_ctx, plan.sub, plan.width)
    return exchange_ctx(mine).reshape(plan.rows, plan.width)


def from_sequences(plan, stack):
    return exchange_ctx(stack.reshape(stack.shape[0], plan.n_ctx, plan.sub, plan.width), 1)


def arranged(plan, moved, *earlier):
    moved = after(moved, *earlier)
    return moved.reshape(moved.shape[0], plan.n_seq, plan.half, plan.width)


def to_output(plan, layers):
    own = by_section(plan, layers[0], layers[1])
    got = other_core(by_section(plan, layers[1], layers[0]))
    first = by_section(plan, own, got)
    second = by_section(plan, got, own)
    both = jnp.stack([first, second], axis=1).astype(F32)
    return both.reshape(1, plan.micro, plan.seqs, plan.span, plan.width)


def shared_keys(plan, own):
    chunks = []
    for mask in range(plan.parts):
        here = own if mask == 0 else xor_ctx(plan, own, mask)
        chunks += [here, other_core(here)]
    return chunks


def return_keys(plan, far):
    got = []
    for mask in range(plan.parts):
        for core in range(2):
            index = 2 * mask + core
            if index == 0:
                continue
            part = far[index - 1]
            if core:
                part = other_core(part)
            if mask:
                part = xor_ctx(plan, part, mask)
            got.append(part)
    return got


def positions_of(plan, section, ctx):
    part = ctx % plan.parts
    start = jnp.arange(plan.n_ctx)[:, None] * plan.span + section * plan.half + part * plan.sub
    return (start + jnp.arange(plan.sub)[None, :]).reshape(-1)


def rope_tables(positions):
    half_width = HD // 2
    frequency = jnp.power(10000.0, -(jnp.arange(half_width).astype(F32) * 2.0) / HD)
    angles = positions.astype(F32)[:, None] * frequency[None, :]
    cos, sin = jnp.cos(angles), jnp.sin(angles)
    return jnp.concatenate([cos] * 4, axis=1), jnp.concatenate([-sin, sin, -sin, sin], axis=1)


def local(tokens, upstream, lengths, w_qkv, w_out, w_in, w_back, gain_attn, gain_ffn):
    plan = Plan(tokens, w_in)
    width = plan.width
    layers = 2

    qkv_low, out_low = w_qkv[0].astype(BF16), w_out[0].astype(BF16)
    in_low, back_low = w_in[0].astype(BF16), to_lanes_of_halves(w_back[0].astype(BF16))
    both = jnp.stack([gain_attn[0], gain_ffn[0]], axis=1).astype(BF16)
    both = jnp.pad(both, ((0, 0), (0, GAIN_LANES - 2)))
    here, there = plan.section, 1 - plan.section

    def attn_half(which):
        value = jnp.where(which == 0, qkv_low[:, 2 * width :], out_low)
        return jnp.concatenate([take_half(plan, qkv_low[:, : 2 * width], which), value, both], axis=1)

    def ffn_half(which):
        return jnp.concatenate(
            [take_half(plan, in_low, which), take_half(plan, back_low, which)], axis=1
        )

    def shards_of(half):
        kept, got = half(here), other_core(half(there))
        return by_section(plan, kept, got), by_section(plan, got, kept)

    attn_shards, ffn_shards = shards_of(attn_half), shards_of(ffn_half)
    tall = 4 * (width // 2)
    if plan.staged:
        attn0_z = spread_ctx(plan, attn_shards[0])
        attn0_dp = SpreadDp(plan, attn0_z)
        ffn0_z = spread_ctx(plan, after(ffn_shards[0], attn0_z))
        source = to_sequences(plan, after(tokens, ffn0_z))
        attn1 = gather_natural(plan, after(attn_shards[1], attn0_z), tall)
        attn0 = attn0_dp.result(ffn0_z)
        ffn0_dp = SpreadDp(plan, ffn0_z, *attn0_dp.got)
        ffn1 = gather_natural(plan, after(ffn_shards[1], attn0_z), tall)
    else:
        source = to_sequences(plan, tokens)
        attn0, attn1 = (gather_natural(plan, shard) for shard in attn_shards)
        ffn0, ffn1 = (gather_natural(plan, shard, tall) for shard in ffn_shards)
    attn0.share()

    cos, sin = rope_tables(positions_of(plan, plan.section, plan.ctx))
    sequence = plan.ctx // plan.parts
    length = lax.dynamic_index_in_dim(lengths.reshape(-1), sequence, 0, keepdims=False)
    places = []
    for mask in range(plan.parts):
        for core in range(2):
            places.append(positions_of(plan, plan.section ^ core, plan.ctx ^ mask))
    hidden_key = jnp.where(jnp.concatenate(places) < length, 0.0, MASKED)
    lane = jnp.arange(PAIR)
    bias = jnp.where(lane[None, :] == 0, hidden_key[:, None], 0.0).astype(BF16)

    order = Order()
    saved, acts, gains = [], [], []

    def forward_qkv(x, attn):
        a, query, own_kv, rows = qkv_forward(plan, order.gate(x), cos, sin, attn)
        order.mark(query)
        gains.append(rows)
        return a, query, shared_keys(plan, own_kv)

    def forward_attention(query, kv):
        out = attention_forward(plan, order.gate(query), kv, bias)
        order.mark(out[2])
        return out

    def forward_ffn(x, layer, attn, ffn, held):
        a, query, kv, o, ot, lse = held
        u2, b, result, low, h, slope = ffn_forward(
            plan, order.gate(o), x, gains[layer], attn, ffn
        )
        order.mark(low)
        saved.append((x, a, query, kv, o, ot, lse, u2, b, h, slope))
        acts.append(low)
        return result

    held = forward_qkv(source, attn0)
    held += tuple(forward_attention(*held[1:]))
    if plan.staged:
        ffn0 = ffn0_dp.result(held[5])
    ffn0.share(held[5])
    attn1.share(held[5])
    x = forward_ffn(source, 0, attn0, ffn0, held)
    held = forward_qkv(x, attn1)
    ffn1.share(held[1])
    held += tuple(forward_attention(*held[1:]))
    cotangent = to_sequences(plan, after(upstream, held[1]))
    forward_ffn(x, 1, attn1, ffn1, held)
    weights = [(attn0, ffn0), (attn1, ffn1)]

    hidden_half, width_half = plan.hidden // 2, width // 2
    grads, dgains = [None] * layers, [None] * layers

    def ffn_part(layer, c):
        attn, ffn = weights[layer]
        u2, _, _, slope = saved[layer][7:]
        out = ffn_backward(plan, order.gate(c), slope, u2, gains[layer], attn, ffn)
        order.mark(out[-1])
        return out

    def attention_part(layer, do):
        x, a, query, kv, o, ot, lse, u2, b, h, slope = saved[layer]
        dq, dk, dv, *far = attention_backward(plan, query, order.gate(do), o, lse, bias, kv)
        order.mark(dq)
        return dq, dk, dv, return_keys(plan, far)

    def qkv_part(layer, dq, dk, dv, far, du2, dg2):
        x = saved[layer][0]
        dqkv, dx, low, dg1 = qkv_backward(
            plan, order.gate(dq), dk, dv, far, du2, x, gains[layer], cos, sin, weights[layer][0]
        )
        order.mark(dg1)
        grads[layer] = low
        dgains[layer] = (dg1, dg2)
        return dqkv, dx, low

    def job_in(left, right):
        return Job(left, right, 0, hidden_half)

    def job_out(left, right):
        return Job(left, right, 0, width_half)

    def job_back(left, right):
        return Job(left, right, 0, width_half, tall=True)

    def job_qkv(left, right):
        return Job(left, right, 0, 3 * width // 2)

    a1, ot1, b1, h1 = (saved[1][i] for i in (1, 5, 8, 9))
    a0, ot0, b0, h0 = (saved[0][i] for i in (1, 5, 8, 9))

    cf, dhp, du2, dz, do, dg2 = ffn_part(1, cotangent)
    sum_ffn1 = WeightGrads(
        plan, [b1, ot1, h1], [dhp, dz, cf], [job_in(0, 0), job_out(1, 1), job_back(2, 2)], False
    )
    sum_ffn1.theirs(order)
    back = attention_part(1, do)
    sum_ffn1.mine(order)
    dqkv, c, low = qkv_part(1, *back, du2, dg2)
    early = from_sequences(plan, jnp.stack([acts[0], acts[1], grads[1]]))
    sum_mixed = WeightGrads(plan, [a1, h0], [dqkv, low], [job_qkv(0, 0), job_back(1, 1)], True)
    sum_mixed.theirs(order)
    sum_mixed.mine(order)
    cf, dhp, du2, dz, do, dg2 = ffn_part(0, c)
    sum_in0 = WeightGrads(plan, [b0, ot0], [dhp, dz], [job_in(0, 0), job_out(1, 1)], True)
    sum_in0.theirs(order)
    sum_in0.mine(order)
    sum_mixed.step("first", order)
    sum_mixed.step("second", order)
    back = attention_part(0, do)
    dqkv, c, low = qkv_part(0, *back, du2, dg2)
    rows = jnp.concatenate([row for pair in dgains for row in pair], axis=0)
    columns = jnp.pad(rows.T, ((0, 0), (0, GAIN_LANES - 2 * layers)))
    sum_qkv0 = WeightGrads(
        plan, [a0, columns], [dqkv], [job_qkv(0, 0), Job(1, None, 0, GAIN_LANES)], True
    )
    sum_qkv0.theirs(order)
    sum_qkv0.mine(order)
    late = from_sequences(plan, order.gate(grads[0])[None])
    sum_in0.step("second", order)
    sum_qkv0.step("second", order)
    early = arranged(plan, early, *order.earlier)
    late = arranged(plan, late, *order.earlier)

    cut = hidden_half + width_half
    ffn1_sum, mixed_sum = sum_ffn1.result(), sum_mixed.result()
    in0_sum, qkv0_sum = sum_in0.result(), sum_qkv0.result()
    wide = 3 * width // 2
    gain_sums = lax.dynamic_slice_in_dim(qkv0_sum[:, wide:], plan.section * 2, 2, axis=1).T.astype(F32)
    sums = [
        (qkv0_sum[:, :wide], in0_sum[:, hidden_half:], in0_sum[:, :hidden_half], from_lanes(mixed_sum[:, wide:])),
        (
            mixed_sum[:, :wide],
            ffn1_sum[:, hidden_half:cut],
            ffn1_sum[:, :hidden_half],
            from_lanes(ffn1_sum[:, cut:]),
        ),
    ]

    def to_owner(first, second):
        own = by_section(plan, first, second)
        got = other_core(by_section(plan, second, first))
        left, right = by_section(plan, own, got), by_section(plan, got, own)
        return jnp.concatenate([left, right], axis=1).astype(F32)[None]

    weight_grads = [to_owner(one, two) for one, two in zip(*sums)]
    return (
        to_output(plan, early[:2]),
        to_output(plan, [late[0], early[2]]),
        *weight_grads,
        gain_sums[0:1],
        gain_sums[1:2],
    )


def solution(mesh):
    rows = P(None, "dp", "ctx", None)
    weight = P("section", ("dp", "ctx"), None)
    gain = P("section", ("dp", "ctx"))
    out_rows = P("section", None, "dp", "ctx", None)
    return jax.shard_map(
        local,
        mesh=mesh,
        in_specs=(rows, rows, P(None, "dp"), weight, weight, weight, weight, gain, gain),
        out_specs=(out_rows, out_rows, weight, weight, weight, weight, gain, gain),
        check_vma=False,
    )
```

```python
import functools

import jax
import jax.numpy as jnp
from jax import lax
from jax.experimental import pallas as pl
from jax.experimental.pallas import tpu as pltpu
from jax.sharding import PartitionSpec as P

HD = 64
PAIR = 2 * HD
BF16 = jnp.bfloat16
F32 = jnp.float32
MASKED = -1e30
COST_SHARE = 0.1
GAIN_LANES = 128


def nn(left, right):
    return lax.dot_general(left, right, (((1,), (0,)), ((), ())), preferred_element_type=F32)


def nt(left, right):
    return lax.dot_general(left, right, (((1,), (1,)), ((), ())), preferred_element_type=F32)


def tn(left, right):
    return lax.dot_general(left, right, (((0,), (0,)), ((), ())), preferred_element_type=F32)


def normalise(rows):
    centred = rows - jnp.mean(rows, axis=-1, keepdims=True)
    scale = lax.rsqrt(jnp.mean(centred * centred, axis=-1, keepdims=True) + 1e-05)
    return centred * scale, scale


def norm_back(rows, gain, grad):
    normed, scale = normalise(rows)
    inner = grad * gain
    mean_inner = jnp.mean(inner, axis=-1, keepdims=True)
    mean_along = jnp.mean(inner * normed, axis=-1, keepdims=True)
    grad_rows = scale * (inner - mean_inner - normed * mean_along)
    return grad_rows, jnp.sum(grad * normed, axis=0, keepdims=True)


def swap_halves(pair_block):
    lane = lax.broadcasted_iota(jnp.int32, pair_block.shape, 1)
    ahead = pltpu.roll(pair_block, PAIR - HD // 2, 1)
    behind = pltpu.roll(pair_block, HD // 2, 1)
    return jnp.where(lane % HD < HD // 2, ahead, behind)


class Plan:
    def __init__(self, tokens, w_in):
        micro, seqs, span, width = tokens.shape
        self.width = width
        self.hidden = w_in.shape[-1]
        self.heads = width // HD
        self.pairs = width // PAIR
        self.n_ctx = lax.axis_size("ctx")
        self.n_dp = lax.axis_size("dp")
        self.micro, self.seqs, self.span = micro, seqs, span
        self.n_seq = micro * seqs
        self.parts = self.n_ctx // self.n_seq
        assert self.parts * self.n_seq == self.n_ctx
        self.half = span // 2
        self.sub = self.half // self.parts
        self.rows = self.n_ctx * self.sub
        self.section = lax.axis_index("section")
        self.dp = lax.axis_index("dp")
        self.ctx = lax.axis_index("ctx")
        self.staged = w_in.shape[1] % 16 == 0 and self.n_ctx == 4 and self.n_dp == 4
        self.blocks = self.n_dp if self.staged else 1
        self.shards = self.n_dp * self.n_ctx if self.staged else 1
        self.shard_rows = width // self.shards
        self.meta = jnp.stack([self.section, self.dp]).astype(jnp.int32)


X_BIT, Y_BIT = 1, 2


def other_core(value):
    return lax.ppermute(value, "section", [(0, 1), (1, 0)])


def xor_dp(plan, value, mask):
    return lax.ppermute(value, "dp", [(i, i ^ mask) for i in range(plan.n_dp)])


def xor_ctx(plan, value, mask):
    return lax.ppermute(value, "ctx", [(i, i ^ mask) for i in range(plan.n_ctx)])


def exchange_ctx(value, dim=0):
    return lax.all_to_all(value, "ctx", dim, dim, tiled=True)


def spread_ctx(plan, shard):
    return exchange_ctx(jnp.concatenate([shard] * plan.n_ctx, axis=0))


def after(value, *earlier):
    earlier = [item for item in earlier if item is not None]
    if not earlier:
        return value
    return lax.optimization_barrier((value, *earlier))[0]


class Spread:
    def __init__(self, own, relative):
        self.own, self.relative = own, relative

    def share(self, *earlier):
        self.other = other_core(after(self.own, *earlier))

    def refs(self):
        return [self.own, self.other]


def to_lanes_of_halves(tall):
    half = tall.shape[1] // 2
    return jnp.concatenate([to_lanes(tall[:, :half]), to_lanes(tall[:, half:])], axis=1)


def to_lanes(tall):
    rows = tall.shape[0] // 4
    return jnp.concatenate([tall[i * rows : (i + 1) * rows] for i in range(4)], axis=1)


def from_lanes(wide):
    cols = wide.shape[1] // 4
    return jnp.concatenate([wide[:, i * cols : (i + 1) * cols] for i in range(4)], axis=0)


def gather_natural(plan, shard, tall=0):
    gathered = lax.all_gather(shard, ("dp", "ctx"), axis=0, tiled=True)
    if plan.staged:
        return Spread(gathered.reshape(plan.shards, plan.shard_rows, -1), False)
    if tall:
        cut = gathered.shape[1] - tall
        n = plan.n_dp * plan.n_ctx
        quarters = gathered[:, cut:].reshape(n, plan.width // n, 4, tall // 4).transpose(0, 2, 1, 3)
        gathered = jnp.concatenate([gathered[:, :cut], to_lanes(quarters.reshape(-1, tall // 4))], axis=1)
    return Spread(gathered[None], False)


class SpreadDp:
    def __init__(self, plan, block, *earlier):
        self.plan = plan
        self.block = after(block, *earlier)
        self.got = [xor_dp(plan, self.block, mask) for mask in (X_BIT, Y_BIT, X_BIT | Y_BIT)]

    def result(self, *earlier):
        plan = self.plan
        blocks = jnp.stack([after(self.block, *earlier), *self.got])
        return Spread(blocks.reshape(plan.shards, plan.shard_rows, -1), True)


class Collect:
    def __init__(self, plan, blocks):
        self.plan = plan
        self.blocks = [blocks[0]] + [xor_dp(plan, blocks[mask], mask) for mask in range(1, plan.n_dp)]

    def first(self, order):
        order.need(*self.blocks[1:])

    def second(self, order):
        plan = self.plan
        own = order.gate(self.blocks[0])
        block = sum(value.astype(F32) for value in [own, *self.blocks[1:]]).astype(BF16)
        order.mark(block)
        self.parts = exchange_ctx(block.reshape(plan.n_ctx, plan.shard_rows, -1))

    def last(self, order):
        order.need(self.parts)

    def result(self):
        return jnp.sum(self.parts.astype(F32), axis=0).astype(BF16)


def smem():
    return pl.BlockSpec(memory_space=pltpu.SMEM)


def anywhere():
    return pl.BlockSpec(memory_space=pl.ANY)


def whole(shape):
    return pl.BlockSpec(shape, lambda i: (0,) * len(shape))


def rows_of(step, width):
    return pl.BlockSpec((step, width), lambda i: (i, 0))


def params(megabytes):
    return pltpu.CompilerParams(vmem_limit_bytes=megabytes * 1024 * 1024)


def cost(flops, bytes_accessed, transcendentals=0):
    return pl.CostEstimate(
        flops=int(flops * COST_SHARE),
        bytes_accessed=int(bytes_accessed * COST_SHARE),
        transcendentals=int(transcendentals * COST_SHARE),
    )


def block_copies(meta, ref, relative, place, lanes, sems, first):
    blocks = 4 if relative else 1
    count = ref.shape[0] // blocks
    copies = []
    for mask in range(blocks):
        start = (meta[1] ^ mask) * count if relative else 0
        copies.append(
            pltpu.make_async_copy(
                ref.at[pl.ds(mask * count, count), :, lanes],
                place(pl.ds(start, count)),
                sems.at[first + mask],
            )
        )
    return copies


def run(copies):
    for copy in copies:
        copy.start()


def wait(copies):
    for copy in copies:
        copy.wait()


class Loads:
    def __init__(self, section, own, other, carrier=None):
        self.section, self.own, self.other, self.carrier = section, own, other, carrier

    def each(self, act):
        if self.carrier is None:
            act(self.own)
            act(self.other)
            return
        pl.when(self.section == self.carrier)(lambda: act(self.own))
        pl.when(self.section != self.carrier)(lambda: act(self.other))

    def start(self):
        self.each(run)

    def wait(self):
        self.each(wait)


def split_refs(refs, counts):
    out, at = [], 0
    for count in counts:
        out.append(refs[at : at + count])
        at += count
    return out


def side(which, half):
    return pl.ds(pl.multiple_of(which * half, 128), half)


def load_halves(meta, relative, refs, matrix, start, sems, first):
    half = matrix.shape[-1] // 2
    lanes = slice(start, start + half)

    def at(which):
        return lambda shards: matrix.at[shards, :, side(which, half)]

    own = block_copies(meta, refs[0], relative, at(meta[0]), lanes, sems, first)
    other = block_copies(meta, refs[1], relative, at(1 - meta[0]), lanes, sems, first + 4)
    return Loads(meta[0], own, other)


def load_tall(meta, relative, refs, matrix, start, sems, first):
    half = matrix.shape[-1] // 2
    own, other = [], []
    for quarter in range(4):
        lanes = slice(start + quarter * half, start + (quarter + 1) * half)

        def at(which, quarter=quarter):
            return lambda shards: matrix.at[shards, quarter, :, side(which, half)]

        where = first + 8 * quarter
        own += block_copies(meta, refs[0], relative, at(meta[0]), lanes, sems, where)
        other += block_copies(meta, refs[1], relative, at(1 - meta[0]), lanes, sems, where + 4)
    return Loads(meta[0], own, other)


def load_one(meta, relative, refs, matrix, start, sems, first, carrier):
    lanes = slice(start, start + matrix.shape[-1])

    def at(shards):
        return matrix.at[shards]

    own = block_copies(meta, refs[0], relative, at, lanes, sems, first)
    other = block_copies(meta, refs[1], relative, at, lanes, sems, first)
    return Loads(meta[0], own, other, carrier)


def flat(matrix):
    return matrix.reshape(-1, matrix.shape[-1])


def row_step(rows, step=128):
    return step if rows % step == 0 else rows


def qkv_kernel(relative, meta, x_ref, cos_ref, sin_ref, *refs):
    attn_refs, rest = split_refs(refs, (2, len(refs) - 2))
    a_ref, q_ref, kv_ref, gains_ref, wqk, wv, columns, sems = rest
    width = wv.shape[-1]
    qk = load_halves(meta, relative, attn_refs, wqk, 0, sems, 0)
    v = load_one(meta, relative, attn_refs, wv, width, sems, 8, 0)
    gain = load_one(meta, relative, attn_refs, columns, 2 * width, sems, 12, 0)
    first = pl.program_id(0) == 0

    @pl.when(first)
    def _():
        gain.start()
        qk.start()
        v.start()
        gain.wait()
        gains_ref[...] = jnp.transpose(flat(columns[...]).astype(F32))[:8]

    normed, _ = normalise(x_ref[...].astype(F32))
    a = (normed * gains_ref[0:1, :]).astype(BF16)
    a_ref[...] = jnp.transpose(a)

    @pl.when(first)
    def _():
        qk.wait()
        v.wait()

    cos, sin = cos_ref[...], sin_ref[...]
    for which in range(2):
        out = nn(a, flat(wqk[:, :, which * width : (which + 1) * width]))
        for pair in range(width // PAIR):
            lanes = slice(pair * PAIR, (pair + 1) * PAIR)
            block = out[:, lanes]
            turned = block * cos + swap_halves(block) * sin
            if which == 0:
                q_ref[:, lanes] = (turned * HD**-0.5).astype(BF16)
            else:
                kv_ref[0, :, lanes] = turned.astype(BF16)
    kv_ref[1] = nn(a, flat(wv[...])).astype(BF16)


def qkv_forward(plan, x, cos, sin, attn):
    rows, width = x.shape
    step = row_step(rows)
    return pl.pallas_call(
        functools.partial(qkv_kernel, attn.relative),
        out_shape=[
            jax.ShapeDtypeStruct((width, rows), BF16),
            jax.ShapeDtypeStruct((rows, width), BF16),
            jax.ShapeDtypeStruct((2, rows, width), BF16),
            jax.ShapeDtypeStruct((8, width), F32),
        ],
        grid=(rows // step,),
        in_specs=[smem(), rows_of(step, width), rows_of(step, PAIR), rows_of(step, PAIR)]
        + [anywhere()] * 2,
        out_specs=[
            pl.BlockSpec((width, step), lambda i: (0, i)),
            rows_of(step, width),
            pl.BlockSpec((2, step, width), lambda i: (0, i, 0)),
            whole((8, width)),
        ],
        scratch_shapes=[
            pltpu.VMEM((plan.shards, plan.shard_rows, 2 * width), BF16),
            pltpu.VMEM((plan.shards, plan.shard_rows, width), BF16),
            pltpu.VMEM((plan.shards, plan.shard_rows, GAIN_LANES), BF16),
            pltpu.SemaphoreType.DMA((16,)),
        ],
        compiler_params=params(56),
        cost_estimate=cost(6 * rows * width * width, 12 * rows * width + 6 * width * width),
        name="qkv_forward",
    )(plan.meta, x, cos, sin, *attn.refs())


def lane_mask(shape, head):
    lane = lax.broadcasted_iota(jnp.int32, shape, 1)
    return lane < HD if head == 0 else lane >= HD


def with_ones(query):
    lane = lax.broadcasted_iota(jnp.int32, query.shape, 1)
    return jnp.concatenate([query, jnp.where(lane == 0, 1.0, 0.0).astype(BF16)], axis=1)


def attention_kernel(chunks, key_block, q_ref, *refs):
    kv = refs[:chunks]
    bias_ref, o_ref, ot_ref, lse_ref, s_scr, vt_scr = refs[chunks:]
    rows = q_ref.shape[0]
    per_chunk = rows // key_block
    query = q_ref[...]
    for c in range(chunks):
        vt_scr[:, c * rows : (c + 1) * rows] = jnp.transpose(kv[c][1])
    outs = []
    for head in range(2):
        extended = with_ones(jnp.where(lane_mask(query.shape, head), query, jnp.zeros_like(query)))
        peak = jnp.full((1, rows), -jnp.inf, F32)
        for c in range(chunks):
            for j in range(per_chunk):
                at = slice(j * key_block, (j + 1) * key_block)
                everywhere = slice(c * rows + at.start, c * rows + at.stop)
                keys = jnp.concatenate([kv[c][0, at, :], bias_ref[everywhere, :]], axis=1)
                scores = nt(keys, extended)
                s_scr[everywhere, :] = scores
                peak = jnp.maximum(peak, jnp.max(scores, axis=0, keepdims=True))
        total = jnp.zeros((1, rows), F32)
        out = jnp.zeros((PAIR, rows), F32)
        for c in range(chunks):
            for j in range(per_chunk):
                everywhere = slice(c * rows + j * key_block, c * rows + (j + 1) * key_block)
                weights = jnp.exp(s_scr[everywhere, :] - peak)
                total = total + jnp.sum(weights, axis=0, keepdims=True)
                out = out + nn(vt_scr[:, everywhere], weights.astype(BF16))
        lse_ref[0, head : head + 1, :] = peak + jnp.log(total)
        outs.append(out / total)
    row = lax.broadcasted_iota(jnp.int32, outs[0].shape, 0)
    out = jnp.where(row < HD, outs[0], outs[1])
    o_ref[...] = jnp.transpose(out).astype(BF16)
    ot_ref[...] = out.astype(BF16)


def attention_forward(plan, query, kv, bias):
    rows, width = query.shape
    chunks = len(kv)
    keys = chunks * rows
    pair_block = pl.BlockSpec((rows, PAIR), lambda p: (0, p))
    kv_block = pl.BlockSpec((2, rows, PAIR), lambda p: (0, 0, p))
    return pl.pallas_call(
        functools.partial(attention_kernel, chunks, min(256, rows)),
        out_shape=[
            jax.ShapeDtypeStruct((rows, width), BF16),
            jax.ShapeDtypeStruct((width, rows), BF16),
            jax.ShapeDtypeStruct((plan.pairs, 8, rows), F32),
        ],
        grid=(plan.pairs,),
        in_specs=[pair_block] + [kv_block] * chunks + [pl.BlockSpec((keys, PAIR), lambda p: (0, 0))],
        out_specs=[
            pair_block,
            pl.BlockSpec((PAIR, rows), lambda p: (p, 0)),
            pl.BlockSpec((1, 8, rows), lambda p: (p, 0, 0)),
        ],
        scratch_shapes=[pltpu.VMEM((keys, rows), F32), pltpu.VMEM((PAIR, keys), BF16)],
        compiler_params=params(56),
        cost_estimate=cost(
            16 * rows * keys * width, 4 * rows * width + 4 * keys * width, rows * keys * plan.heads
        ),
        name="attention_forward",
    )(query, *kv, bias)


def layer_loads(meta, relative, attn_refs, ffn_refs, wo, w1, w2, sems):
    half = w1.shape[-1] // 2
    out = load_one(meta, relative[0], attn_refs, wo, wo.shape[-1], sems, 0, 1)
    first = load_halves(meta, relative[1], ffn_refs, w1, 0, sems, 4)
    second = load_tall(meta, relative[1], ffn_refs, w2, half, sems, 12)
    return out, first, second


def layer_scratch(plan):
    width, hidden, n, rows = plan.width, plan.hidden, plan.shards, plan.shard_rows
    return [
        pltpu.VMEM((n, rows, width), BF16),
        pltpu.VMEM((n, rows, hidden), BF16),
        pltpu.VMEM((n, 4, rows, width), BF16),
        pltpu.SemaphoreType.DMA((44,)),
    ]


def tall_chunk(w2, i):
    n = w2.shape[0]
    value = w2[pl.ds(i * (n // 4), n // 4)] if n >= 4 else w2[0, i]
    return flat(value)


def ffn_kernel(relative, meta, o_ref, x_ref, gains_ref, *refs):
    attn_refs, ffn_refs, rest = split_refs(refs, (2, 2, len(refs) - 4))
    u2_ref, bt_ref, acts_ref, low_ref, ht_ref, slope_ref, wo, w1, w2, sems, b_ref = rest
    out, first, second = layer_loads(meta, relative, attn_refs, ffn_refs, wo, w1, w2, sems)
    chunk = slope_ref.shape[1]
    i = pl.program_id(0)

    @pl.when(i == 0)
    def _():
        out.start()
        first.start()
        second.start()
        out.wait()
        u2 = x_ref[...].astype(F32) + nn(o_ref[...], flat(wo[...]))
        u2_ref[...] = u2
        acts_ref[...] = u2
        b = (normalise(u2)[0] * gains_ref[1:2, :]).astype(BF16)
        b_ref[...] = b
        bt_ref[...] = jnp.transpose(b)
        first.wait()
        second.wait()

    at = pl.ds(pl.multiple_of(i * chunk, chunk), chunk)
    hp = nn(b_ref[...], flat(w1[:, :, at]))
    cdf = 0.5 * (1.0 + lax.erf(hp * (0.5**0.5)))
    density = jnp.exp(-0.5 * hp * hp) * 0.3989422804014327
    h = (hp * cdf).astype(BF16)
    ht_ref[...] = jnp.transpose(h)
    slope_ref[...] = (cdf + hp * density).astype(BF16)
    acts_ref[...] += nn(h, tall_chunk(w2, i))

    @pl.when(i == pl.num_programs(0) - 1)
    def _():
        low_ref[...] = acts_ref[...].astype(BF16)


def ffn_forward(plan, o, x, gains, attn, ffn):
    rows, width = x.shape
    hidden = plan.hidden
    chunk = hidden // 4
    refs = [*attn.refs(), *ffn.refs()]
    relative = (attn.relative, ffn.relative)
    columns = pl.BlockSpec((rows, chunk), lambda i: (0, i))
    return pl.pallas_call(
        functools.partial(ffn_kernel, relative),
        out_shape=[
            jax.ShapeDtypeStruct((rows, width), F32),
            jax.ShapeDtypeStruct((width, rows), BF16),
            jax.ShapeDtypeStruct((rows, width), F32),
            jax.ShapeDtypeStruct((rows, width), BF16),
            jax.ShapeDtypeStruct((hidden, rows), BF16),
            jax.ShapeDtypeStruct((rows, hidden), BF16),
        ],
        grid=(hidden // chunk,),
        in_specs=[smem(), whole((rows, width)), whole((rows, width)), whole((8, width))]
        + [anywhere()] * len(refs),
        out_specs=[whole((rows, width)), whole((width, rows)), whole((rows, width)), whole((rows, width))]
        + [rows_of(chunk, rows), columns],
        scratch_shapes=[
            *layer_scratch(plan),
            pltpu.VMEM((rows, width), BF16),
        ],
        compiler_params=params(56),
        cost_estimate=cost(
            4 * rows * width * hidden + 2 * rows * width * width + 60 * rows * hidden,
            20 * rows * width + 4 * rows * hidden + 4 * width * hidden,
            2 * rows * hidden,
        ),
        name="ffn_forward",
    )(plan.meta, o, x, gains, *refs)


def ffn_back_kernel(relative, meta, c_ref, slope_ref, u2_ref, gains_ref, *refs):
    attn_refs, ffn_refs, rest = split_refs(refs, (2, 2, len(refs) - 4))
    cf_ref, dhp_ref, du2_ref, dz_ref, do_ref, dg_ref, send_ref, wo, w1, w2, sems, acc = rest
    out, first, second = layer_loads(meta, relative, attn_refs, ffn_refs, wo, w1, w2, sems)
    chunk = dhp_ref.shape[1]
    i = pl.program_id(0)

    @pl.when(i == 0)
    def _():
        second.start()
        first.start()
        out.start()
        cf_ref[...] = c_ref[...].astype(BF16)
        acc[...] = jnp.zeros_like(acc)
        second.wait()
        first.wait()
        out.wait()

    at = pl.ds(pl.multiple_of(i * chunk, chunk), chunk)
    dh = nt(cf_ref[...], tall_chunk(w2, i))
    dhp = (dh * slope_ref[...].astype(F32)).astype(BF16)
    dhp_ref[...] = dhp
    there = 1 - meta[0]
    steps = pl.num_programs(0) // 2

    @pl.when(i // steps == there)
    def _():
        send_ref[:, pl.ds(pl.multiple_of((i % steps) * chunk, 128), chunk)] = dhp
    acc[...] += nt(dhp, flat(w1[:, :, at]))

    @pl.when(i == pl.num_programs(0) - 1)
    def _():
        grad, dgain = norm_back(u2_ref[...], gains_ref[1:2, :], acc[...])
        du2 = c_ref[...].astype(F32) + grad
        du2_ref[...] = du2
        dg_ref[...] = dgain
        dz = du2.astype(BF16)
        dz_ref[...] = dz
        do_ref[...] = nt(dz, flat(wo[...])).astype(BF16)
        half = dz.shape[1] // 2
        begin = send_ref.shape[1] - 2 * half
        send_ref[:, begin : begin + half] = dz_ref[:, side(there, half)]
        send_ref[:, begin + half :] = cf_ref[:, side(there, half)]


def ffn_backward(plan, c, slope, u2, gains, attn, ffn):
    rows, width = u2.shape
    hidden = plan.hidden
    chunk = hidden // 4
    refs = [*attn.refs(), *ffn.refs()]
    relative = (attn.relative, ffn.relative)
    columns = pl.BlockSpec((rows, chunk), lambda i: (0, i))
    wide = jax.ShapeDtypeStruct((rows, width), BF16)
    full = whole((rows, width))
    return pl.pallas_call(
        functools.partial(ffn_back_kernel, relative),
        out_shape=[
            wide,
            jax.ShapeDtypeStruct((rows, hidden), BF16),
            jax.ShapeDtypeStruct((rows, width), F32),
            wide,
            wide,
            jax.ShapeDtypeStruct((1, width), F32),
            jax.ShapeDtypeStruct((rows, hidden // 2 + width), BF16),
        ],
        grid=(hidden // chunk,),
        in_specs=[smem(), full, columns, full, whole((8, width))] + [anywhere()] * len(refs),
        out_specs=[full, columns, full, full, full, whole((1, width)), whole((rows, hidden // 2 + width))],
        scratch_shapes=[
            *layer_scratch(plan),
            pltpu.VMEM((rows, width), F32),
        ],
        compiler_params=params(56),
        cost_estimate=cost(
            4 * rows * width * hidden + 2 * rows * width * width,
            18 * rows * width + 4 * rows * hidden + 4 * width * hidden + 2 * width * width,
        ),
        name="ffn_backward",
    )(plan.meta, c, slope, u2, gains, *refs)


def attention_back_kernel(chunks, key_block, q_ref, do_ref, o_ref, lse_ref, bias_ref, *refs):
    kv = refs[:chunks]
    dq_ref, dk_ref, dv_ref = refs[chunks : chunks + 3]
    far = refs[chunks + 3 : 2 * chunks + 2]
    kt_scr, dk_scr, dv_scr = refs[2 * chunks + 2 :]
    rows = q_ref.shape[0]
    per_chunk = rows // key_block
    query, grad = q_ref[...], do_ref[...]
    for c in range(chunks):
        kt_scr[:, c * rows : (c + 1) * rows] = jnp.transpose(kv[c][0])
    products = jnp.transpose(grad.astype(F32) * o_ref[...].astype(F32))
    outs = []
    for head in range(2):
        mask = lane_mask(query.shape, head)
        masked_query = jnp.where(mask, query, jnp.zeros_like(query))
        masked_grad = jnp.where(mask, grad, jnp.zeros_like(grad))
        extended = with_ones(masked_query)
        delta = jnp.sum(products[head * HD : (head + 1) * HD], axis=0, keepdims=True)
        lse = lse_ref[0, head : head + 1, :]
        dqt = jnp.zeros((PAIR, rows), F32)
        for c in range(chunks):
            for j in range(per_chunk):
                at = slice(j * key_block, (j + 1) * key_block)
                everywhere = slice(c * rows + at.start, c * rows + at.stop)
                keys = jnp.concatenate([kv[c][0, at, :], bias_ref[everywhere, :]], axis=1)
                weights = jnp.exp(nt(keys, extended) - lse)
                grad_weights = nt(kv[c][1, at, :], masked_grad)
                grad_scores = (weights * (grad_weights - delta)).astype(BF16)
                dv = nn(weights.astype(BF16), masked_grad)
                dk = nn(grad_scores, masked_query)
                dqt = dqt + nn(kt_scr[:, everywhere], grad_scores)
                if head == 0:
                    dv_scr[everywhere, :] = dv
                    dk_scr[everywhere, :] = dk
                elif c == 0:
                    dk_ref[at, :] = dk_scr[everywhere, :] + dk
                    dv_ref[at, :] = dv_scr[everywhere, :] + dv
                else:
                    far[c - 1][0, at, :] = (dk_scr[everywhere, :] + dk).astype(BF16)
                    far[c - 1][1, at, :] = (dv_scr[everywhere, :] + dv).astype(BF16)
        outs.append(dqt)
    row = lax.broadcasted_iota(jnp.int32, outs[0].shape, 0)
    dq_ref[...] = jnp.transpose(jnp.where(row < HD, outs[0], outs[1])).astype(BF16)


def attention_backward(plan, query, grad, o, lse, bias, kv):
    rows, width = query.shape
    chunks = len(kv)
    keys = chunks * rows
    pair_block = pl.BlockSpec((rows, PAIR), lambda p: (0, p))
    kv_block = pl.BlockSpec((2, rows, PAIR), lambda p: (0, 0, p))
    near = jax.ShapeDtypeStruct((rows, width), F32)
    return pl.pallas_call(
        functools.partial(attention_back_kernel, chunks, min(256, rows)),
        out_shape=[jax.ShapeDtypeStruct((rows, width), BF16), near, near]
        + [jax.ShapeDtypeStruct((2, rows, width), BF16)] * (chunks - 1),
        grid=(plan.pairs,),
        in_specs=[pair_block] * 3
        + [
            pl.BlockSpec((1, 8, rows), lambda p: (p, 0, 0)),
            pl.BlockSpec((keys, PAIR), lambda p: (0, 0)),
        ]
        + [kv_block] * chunks,
        out_specs=[pair_block] * 3 + [kv_block] * (chunks - 1),
        scratch_shapes=[
            pltpu.VMEM((PAIR, keys), BF16),
            pltpu.VMEM((keys, PAIR), F32),
            pltpu.VMEM((keys, PAIR), F32),
        ],
        compiler_params=params(56),
        cost_estimate=cost(
            40 * rows * keys * width,
            16 * rows * width + 8 * keys * width,
            rows * keys * plan.heads,
        ),
        name="attention_backward",
    )(query, grad, o, lse, bias, *kv)


def qkv_back_kernel(
    spread, n_far, meta, dq_ref, dk_ref, dv_ref, du2_ref, x_ref, gains_ref, cos_ref, sin_ref, *refs
):
    far, attn_refs, rest = split_refs(refs, (n_far, len(refs) - n_far - 8, 8))
    dqkv_ref, dx_ref, low_ref, dg_ref, send_ref, wqk, wv, sems = rest
    qk = load_halves(meta, spread, attn_refs, wqk, 0, sems, 0)
    v = load_one(meta, spread, attn_refs, wv, wv.shape[-1], sems, 8, 0)
    first = pl.program_id(0) == 0

    @pl.when(first)
    def _():
        qk.start()
        v.start()
        dg_ref[...] = jnp.zeros_like(dg_ref)

    width = x_ref.shape[1]
    cos, sin = cos_ref[...], sin_ref[...]
    for pair in range(width // PAIR):
        lanes = slice(pair * PAIR, (pair + 1) * PAIR)
        dq = dq_ref[:, lanes].astype(F32) * HD**-0.5
        dk, dv = dk_ref[:, lanes], dv_ref[:, lanes]
        for part in far:
            dk = dk + part[0, :, lanes].astype(F32)
            dv = dv + part[1, :, lanes].astype(F32)
        dk = dk.astype(BF16).astype(F32)
        dqkv_ref[:, pair * PAIR : (pair + 1) * PAIR] = (dq * cos - swap_halves(dq) * sin).astype(BF16)
        at = width + pair * PAIR
        dqkv_ref[:, at : at + PAIR] = (dk * cos - swap_halves(dk) * sin).astype(BF16)
        at = 2 * width + pair * PAIR
        dqkv_ref[:, at : at + PAIR] = dv.astype(BF16)

    @pl.when(first)
    def _():
        qk.wait()
        v.wait()

    da = nt(dqkv_ref[:, : 2 * width], flat(wqk[...]))
    da = da + nt(dqkv_ref[:, 2 * width :], flat(wv[...]))
    grad, dgain = norm_back(x_ref[...].astype(F32), gains_ref[0:1, :], da)
    dx = du2_ref[...] + grad
    dx_ref[...] = dx
    low_ref[...] = dx.astype(BF16)
    dg_ref[...] += dgain
    there = 1 - meta[0]
    wide = 3 * width // 2
    send_ref[:, :wide] = dqkv_ref[:, side(there, wide)]
    send_ref[:, wide:] = low_ref[:, side(there, width // 2)]


def qkv_backward(plan, dq, dk, dv, far, du2, x, gains, cos, sin, attn):
    rows, width = x.shape
    step = row_step(rows)
    refs = attn.refs()
    some = rows_of(step, width)
    return pl.pallas_call(
        functools.partial(qkv_back_kernel, attn.relative, len(far)),
        out_shape=[
            jax.ShapeDtypeStruct((rows, 3 * width), BF16),
            jax.ShapeDtypeStruct((rows, width), F32),
            jax.ShapeDtypeStruct((rows, width), BF16),
            jax.ShapeDtypeStruct((1, width), F32),
            jax.ShapeDtypeStruct((rows, 2 * width), BF16),
        ],
        grid=(rows // step,),
        in_specs=[smem()]
        + [some] * 5
        + [whole((8, width)), rows_of(step, PAIR), rows_of(step, PAIR)]
        + [pl.BlockSpec((2, step, width), lambda i: (0, i, 0))] * len(far)
        + [anywhere()] * len(refs),
        out_specs=[rows_of(step, 3 * width), some, some, whole((1, width)), rows_of(step, 2 * width)],
        scratch_shapes=[
            pltpu.VMEM((plan.shards, plan.shard_rows, 2 * width), BF16),
            pltpu.VMEM((plan.shards, plan.shard_rows, width), BF16),
            pltpu.SemaphoreType.DMA((12,)),
        ],
        compiler_params=params(56),
        cost_estimate=cost(6 * rows * width * width, 30 * rows * width + 6 * width * width),
        name="qkv_backward",
    )(plan.meta, dq, dk, dv, du2, x, gains, cos, sin, *far, *refs)


class Job:
    def __init__(self, left, right, cols, at=0, tall=False):
        self.left, self.right, self.cols, self.at, self.tall = left, right, cols, at, tall
        self.lanes = 4 * cols if tall else cols


def weight_kernel(jobs, n_lefts, n_rights, relative, meta, *refs):
    lefts, rights, (got,), outs, (acc,) = split_refs(
        refs, (n_lefts, n_rights, 1, len(refs) - n_lefts - n_rights - 2, 1)
    )
    step = pl.program_id(0)
    shards, size = acc.shape[:2]
    lane = 0
    for job in jobs:
        own, other = lefts[job.left], lefts[job.left + 1]
        if job.right is None:
            product = own[...] + other[...]
        else:
            columns = rights[job.right][:, side(meta[0], rights[job.right].shape[1] // 2)]
            product = nn(own[...], columns)
            product = product + nn(other[...], got[:, job.at : job.at + job.cols])
        if job.tall:
            product = product.reshape(shards, 4, size, job.cols)
            for quarter in range(4):
                acc[:, :, lane : lane + job.cols] = product[:, quarter]
                lane += job.cols
        else:
            acc[:, :, lane : lane + job.cols] = product.reshape(shards, size, job.cols)
            lane += job.cols
    if not relative:
        outs[0][0] = acc[...].astype(BF16)
        return
    for mask, out in enumerate(outs):

        @pl.when(step == mask)
        def _(out=out):
            out[...] = acc[...].astype(BF16)


def weight_call(plan, lefts, rights, jobs, got, relative):
    rows = rights[0].shape[0]
    n = plan.blocks
    shape = (plan.shards // n, plan.shard_rows, sum(job.lanes for job in jobs))
    if relative:
        out_shape = [jax.ShapeDtypeStruct(shape, BF16)] * n
        out_specs = [pl.BlockSpec(shape, lambda i, meta: (0, 0, 0))] * n
    else:
        out_shape = [jax.ShapeDtypeStruct((n, *shape), BF16)]
        out_specs = [pl.BlockSpec((1, *shape), lambda i, meta: (i, 0, 0, 0))]

    def block_of(i, meta):
        return (meta[1] ^ i if relative else i, 0)

    def all_of(value):
        return pl.BlockSpec(value.shape, lambda i, meta: (0, 0))

    moved = sum(value.size * 2 for value in [*lefts, *rights, got])
    moved += 2 * n * shape[0] * shape[1] * shape[2]
    flops = sum(
        4 * rows * lefts[job.left].shape[0] * job.cols for job in jobs if job.right is not None
    )
    result = pl.pallas_call(
        functools.partial(weight_kernel, jobs, len(lefts), len(rights), relative),
        out_shape=out_shape,
        grid_spec=pltpu.PrefetchScalarGridSpec(
            num_scalar_prefetch=1,
            grid=(n,),
            in_specs=[
                pl.BlockSpec((value.shape[0] // n, value.shape[1]), block_of) for value in lefts
            ]
            + [all_of(value) for value in [*rights, got]],
            out_specs=out_specs,
            scratch_shapes=[pltpu.VMEM(shape, F32)],
        ),
        compiler_params=params(56),
        cost_estimate=cost(flops, moved),
        name="weight_grads",
    )(plan.meta, *lefts, *rights, got)
    return result if relative else result[0]


class WeightGrads:
    def __init__(self, plan, order, lefts, rights, jobs, got, ahead=None):
        self.plan, self.relative = plan, plan.staged
        lefts = [order.gate(lefts[0]), *lefts[1:]]
        out = weight_call(plan, lefts, rights, jobs, got, self.relative)
        if self.relative:
            order.mark(out[0])
            earlier = ahead.sums.blocks[1:] if ahead else []
            self.sums = Collect(plan, [after(block, *earlier) for block in out])
            return
        order.mark(out)
        tall = sum(job.lanes for job in jobs if job.tall)
        out = out.reshape(plan.width, -1)
        cut = out.shape[1] - tall
        self.total = lax.psum_scatter(out[:, :cut], ("dp", "ctx"), scatter_dimension=0, tiled=True)
        if tall:
            part = from_lanes(out[:, cut:])
            part = lax.psum_scatter(part, ("dp", "ctx"), scatter_dimension=0, tiled=True)
            self.total = jnp.concatenate([self.total, to_lanes(part)], axis=1)

    def step(self, name, order):
        if self.relative:
            getattr(self.sums, name)(order)

    def result(self):
        return self.sums.result() if self.relative else self.total


class Order:
    def __init__(self):
        self.earlier = []

    def gate(self, value):
        return after(value, *self.earlier)

    def mark(self, value):
        self.earlier = [] if value is None else [value]

    def need(self, *values):
        self.earlier += [value for value in values if value is not None]


def by_section(plan, first, second):
    return jnp.where(plan.section == 0, first, second)


def take_half(plan, matrix, which):
    half = matrix.shape[-1] // 2
    return lax.dynamic_slice_in_dim(matrix, which * half, half, axis=matrix.ndim - 1)


def to_sequences(plan, tokens):
    pieces = tokens.reshape(plan.n_seq, 2, plan.half, plan.width)
    mine = lax.dynamic_index_in_dim(pieces, plan.section, 1, keepdims=False)
    mine = mine.reshape(plan.n_ctx, plan.sub, plan.width)
    return exchange_ctx(mine).reshape(plan.rows, plan.width)


def from_sequences(plan, stack):
    return exchange_ctx(stack.reshape(stack.shape[0], plan.n_ctx, plan.sub, plan.width), 1)


def arranged(plan, moved, *earlier):
    moved = after(moved, *earlier)
    return moved.reshape(moved.shape[0], plan.n_seq, plan.half, plan.width)


def to_output(plan, layers):
    own = by_section(plan, layers[0], layers[1])
    got = other_core(by_section(plan, layers[1], layers[0]))
    first = by_section(plan, own, got)
    second = by_section(plan, got, own)
    both = jnp.stack([first, second], axis=1).astype(F32)
    return both.reshape(1, plan.micro, plan.seqs, plan.span, plan.width)


def shared_keys(plan, own):
    chunks = []
    for mask in range(plan.parts):
        here = own if mask == 0 else xor_ctx(plan, own, mask)
        chunks += [here, other_core(here)]
    return chunks


def return_keys(plan, far):
    got = []
    for mask in range(plan.parts):
        for core in range(2):
            index = 2 * mask + core
            if index == 0:
                continue
            part = far[index - 1]
            if core:
                part = other_core(part)
            if mask:
                part = xor_ctx(plan, part, mask)
            got.append(part)
    return got


def positions_of(plan, section, ctx):
    part = ctx % plan.parts
    start = jnp.arange(plan.n_ctx)[:, None] * plan.span + section * plan.half + part * plan.sub
    return (start + jnp.arange(plan.sub)[None, :]).reshape(-1)


def rope_tables(positions):
    half_width = HD // 2
    frequency = jnp.power(10000.0, -(jnp.arange(half_width).astype(F32) * 2.0) / HD)
    angles = positions.astype(F32)[:, None] * frequency[None, :]
    cos, sin = jnp.cos(angles), jnp.sin(angles)
    return jnp.concatenate([cos] * 4, axis=1), jnp.concatenate([-sin, sin, -sin, sin], axis=1)


def local(tokens, upstream, lengths, w_qkv, w_out, w_in, w_back, gain_attn, gain_ffn):
    plan = Plan(tokens, w_in)
    width = plan.width
    layers = 2

    qkv_low, out_low = w_qkv[0].astype(BF16), w_out[0].astype(BF16)
    in_low, back_low = w_in[0].astype(BF16), to_lanes_of_halves(w_back[0].astype(BF16))
    both = jnp.stack([gain_attn[0], gain_ffn[0]], axis=1).astype(BF16)
    both = jnp.pad(both, ((0, 0), (0, GAIN_LANES - 2)))
    here, there = plan.section, 1 - plan.section

    def attn_half(which):
        value = jnp.where(which == 0, qkv_low[:, 2 * width :], out_low)
        return jnp.concatenate([take_half(plan, qkv_low[:, : 2 * width], which), value, both], axis=1)

    def ffn_half(which):
        return jnp.concatenate(
            [take_half(plan, in_low, which), take_half(plan, back_low, which)], axis=1
        )

    def shards_of(half):
        kept, got = half(here), other_core(half(there))
        return by_section(plan, kept, got), by_section(plan, got, kept)

    attn_shards, ffn_shards = shards_of(attn_half), shards_of(ffn_half)
    tall = 4 * (width // 2)
    if plan.staged:
        attn0_z = spread_ctx(plan, attn_shards[0])
        attn0_dp = SpreadDp(plan, attn0_z)
        ffn0_z = spread_ctx(plan, after(ffn_shards[0], attn0_z))
        source = to_sequences(plan, after(tokens, ffn0_z))
        attn1 = gather_natural(plan, after(attn_shards[1], attn0_z), tall)
        attn0 = attn0_dp.result(ffn0_z)
        ffn0_dp = SpreadDp(plan, ffn0_z, *attn0_dp.got)
        ffn1 = gather_natural(plan, after(ffn_shards[1], attn0_z), tall)
    else:
        source = to_sequences(plan, tokens)
        attn0, attn1 = (gather_natural(plan, shard) for shard in attn_shards)
        ffn0, ffn1 = (gather_natural(plan, shard, tall) for shard in ffn_shards)
    attn0.share()

    cos, sin = rope_tables(positions_of(plan, plan.section, plan.ctx))
    sequence = plan.ctx // plan.parts
    length = lax.dynamic_index_in_dim(lengths.reshape(-1), sequence, 0, keepdims=False)
    places = []
    for mask in range(plan.parts):
        for core in range(2):
            places.append(positions_of(plan, plan.section ^ core, plan.ctx ^ mask))
    hidden_key = jnp.where(jnp.concatenate(places) < length, 0.0, MASKED)
    lane = jnp.arange(PAIR)
    bias = jnp.where(lane[None, :] == 0, hidden_key[:, None], 0.0).astype(BF16)

    order = Order()
    saved, acts, gains, others = [], [], [], []

    def forward_qkv(x, attn):
        a, query, own_kv, rows = qkv_forward(plan, order.gate(x), cos, sin, attn)
        order.mark(query)
        gains.append(rows)
        return a, query, shared_keys(plan, own_kv)

    def forward_attention(query, kv):
        out = attention_forward(plan, order.gate(query), kv, bias)
        order.mark(out[2])
        return out

    def forward_ffn(x, layer, attn, ffn, held):
        a, query, kv, o, ot, lse = held
        u2, b, result, low, h, slope = ffn_forward(
            plan, order.gate(o), x, gains[layer], attn, ffn
        )
        order.mark(low)
        saved.append((x, a, query, kv, o, ot, lse, u2, b, h, slope))
        acts.append(low)
        others.append([other_core(value) for value in (a, ot, b, h)])
        return result

    if plan.staged:
        order.need(*ffn0_dp.got[:2])
    held = forward_qkv(source, attn0)
    held += tuple(forward_attention(*held[1:]))
    if plan.staged:
        ffn0 = ffn0_dp.result(held[5])
    ffn0.share(held[5])
    attn1.share(held[5])
    x = forward_ffn(source, 0, attn0, ffn0, held)
    held = forward_qkv(x, attn1)
    held += tuple(forward_attention(*held[1:]))
    ffn1.share(held[5])
    cotangent = to_sequences(plan, after(upstream, held[1]))
    forward_ffn(x, 1, attn1, ffn1, held)
    weights = [(attn0, ffn0), (attn1, ffn1)]

    hidden_half, width_half = plan.hidden // 2, width // 2
    grads, dgains = [None] * layers, [None] * layers

    def ffn_part(layer, c):
        attn, ffn = weights[layer]
        u2, _, _, slope = saved[layer][7:]
        out = ffn_backward(plan, order.gate(c), slope, u2, gains[layer], attn, ffn)
        order.mark(out[5])
        return out

    def attention_part(layer, do):
        x, a, query, kv, o, ot, lse, u2, b, h, slope = saved[layer]
        dq, dk, dv, *far = attention_backward(plan, query, order.gate(do), o, lse, bias, kv)
        order.mark(dq)
        return dq, dk, dv, return_keys(plan, far)

    def qkv_part(layer, dq, dk, dv, far, du2, dg2):
        x = saved[layer][0]
        dqkv, dx, low, dg1, send = qkv_backward(
            plan, order.gate(dq), dk, dv, far, du2, x, gains[layer], cos, sin, weights[layer][0]
        )
        order.mark(dg1)
        grads[layer] = low
        dgains[layer] = (dg1, dg2)
        return dqkv, dx, low, send

    wide = 3 * width // 2
    a1, ot1, b1, h1 = (saved[1][i] for i in (1, 5, 8, 9))
    a0, ot0, b0, h0 = (saved[0][i] for i in (1, 5, 8, 9))
    (far_a0, far_ot0, far_b0, far_h0), (far_a1, far_ot1, far_b1, far_h1) = others

    cf, dhp, du2, dz, do, dg2, send = ffn_part(1, cotangent)
    got = other_core(send)
    acts_back = from_sequences(plan, jnp.stack(acts))
    back = attention_part(1, do)
    sum_ffn1 = WeightGrads(
        plan,
        order,
        [b1, far_b1, ot1, far_ot1, h1, far_h1],
        [dhp, dz, cf],
        [
            Job(0, 0, hidden_half),
            Job(2, 1, width_half, hidden_half),
            Job(4, 2, width_half, hidden_half + width_half, tall=True),
        ],
        got,
    )
    order.need(acts_back)
    dqkv, c, low, send = qkv_part(1, *back, du2, dg2)
    got = other_core(send)
    grads1_back = from_sequences(plan, grads[1][None])
    cf, dhp, du2, dz, do, dg2, send = ffn_part(0, c)
    got_ffn = other_core(send)
    sum_ffn1.step("first", order)
    order.need(grads1_back)
    sum_ffn1.step("second", order)
    sum_mixed = WeightGrads(
        plan,
        order,
        [a1, far_a1, h0, far_h0],
        [dqkv, low],
        [Job(0, 0, wide), Job(2, 1, width_half, wide, tall=True)],
        got,
    )
    sum_in0 = WeightGrads(
        plan,
        order,
        [b0, far_b0, ot0, far_ot0],
        [dhp, dz],
        [Job(0, 0, hidden_half), Job(2, 1, width_half, hidden_half)],
        got_ffn,
        sum_mixed,
    )
    back = attention_part(0, do)
    sum_mixed.step("first", order)
    sum_mixed.step("second", order)
    dqkv, c, low, send = qkv_part(0, *back, du2, dg2)
    got = other_core(send)
    rows = jnp.concatenate([row for pair in dgains for row in pair], axis=0)
    columns = jnp.pad(rows.T, ((0, 0), (0, GAIN_LANES - 2 * layers)))
    sum_in0.step("first", order)
    sum_qkv0 = WeightGrads(
        plan,
        order,
        [a0, far_a0, columns, other_core(columns)],
        [dqkv],
        [Job(0, 0, wide), Job(2, None, GAIN_LANES)],
        got,
    )
    sum_in0.step("second", order)
    grads0_back = from_sequences(plan, order.gate(grads[0])[None])
    acts_back = arranged(plan, acts_back, *order.earlier)
    acts_out = to_output(plan, acts_back)
    sum_qkv0.step("second", order)
    grads0_back = arranged(plan, grads0_back, *order.earlier)
    grads1_back = arranged(plan, grads1_back, *order.earlier)

    cut = hidden_half + width_half
    ffn1_sum, mixed_sum = sum_ffn1.result(), sum_mixed.result()
    in0_sum, qkv0_sum = sum_in0.result(), sum_qkv0.result()
    gain_sums = lax.dynamic_slice_in_dim(qkv0_sum[:, wide:], plan.section * 2, 2, axis=1).T.astype(F32)
    sums = [
        (qkv0_sum[:, :wide], in0_sum[:, hidden_half:], in0_sum[:, :hidden_half], from_lanes(mixed_sum[:, wide:])),
        (
            mixed_sum[:, :wide],
            ffn1_sum[:, hidden_half:cut],
            ffn1_sum[:, :hidden_half],
            from_lanes(ffn1_sum[:, cut:]),
        ),
    ]

    def to_owner(first, second):
        own = by_section(plan, first, second)
        got = other_core(by_section(plan, second, first))
        left, right = by_section(plan, own, got), by_section(plan, got, own)
        return jnp.concatenate([left, right], axis=1).astype(F32)[None]

    weight_grads = [to_owner(one, two) for one, two in zip(*sums)]
    return (
        acts_out,
        to_output(plan, [grads0_back[0], grads1_back[0]]),
        *weight_grads,
        gain_sums[0:1],
        gain_sums[1:2],
    )


def solution(mesh):
    rows = P(None, "dp", "ctx", None)
    weight = P("section", ("dp", "ctx"), None)
    gain = P("section", ("dp", "ctx"))
    out_rows = P("section", None, "dp", "ctx", None)
    return jax.shard_map(
        local,
        mesh=mesh,
        in_specs=(rows, rows, P(None, "dp"), weight, weight, weight, weight, gain, gain),
        out_specs=(out_rows, out_rows, weight, weight, weight, weight, gain, gain),
        check_vma=False,
    )
```

```python
import functools

import jax
import jax.numpy as jnp
from jax import lax
from jax.experimental import pallas as pl
from jax.experimental.pallas import tpu as pltpu
from jax.sharding import PartitionSpec as P

HD = 64
PAIR = 2 * HD
BF16 = jnp.bfloat16
F32 = jnp.float32
MASKED = -1e30
COST_SHARE = 0.1
GAIN_LANES = 128


def nn(left, right):
    return lax.dot_general(left, right, (((1,), (0,)), ((), ())), preferred_element_type=F32)


def nt(left, right):
    return lax.dot_general(left, right, (((1,), (1,)), ((), ())), preferred_element_type=F32)


def tn(left, right):
    return lax.dot_general(left, right, (((0,), (0,)), ((), ())), preferred_element_type=F32)


def normalise(rows):
    centred = rows - jnp.mean(rows, axis=-1, keepdims=True)
    scale = lax.rsqrt(jnp.mean(centred * centred, axis=-1, keepdims=True) + 1e-05)
    return centred * scale, scale


def norm_back(rows, gain, grad):
    normed, scale = normalise(rows)
    inner = grad * gain
    mean_inner = jnp.mean(inner, axis=-1, keepdims=True)
    mean_along = jnp.mean(inner * normed, axis=-1, keepdims=True)
    grad_rows = scale * (inner - mean_inner - normed * mean_along)
    return grad_rows, jnp.sum(grad * normed, axis=0, keepdims=True)


def swap_halves(pair_block):
    lane = lax.broadcasted_iota(jnp.int32, pair_block.shape, 1)
    ahead = pltpu.roll(pair_block, PAIR - HD // 2, 1)
    behind = pltpu.roll(pair_block, HD // 2, 1)
    return jnp.where(lane % HD < HD // 2, ahead, behind)


class Plan:
    def __init__(self, tokens, w_in):
        micro, seqs, span, width = tokens.shape
        self.width = width
        self.hidden = w_in.shape[-1]
        self.heads = width // HD
        self.pairs = width // PAIR
        self.n_ctx = lax.axis_size("ctx")
        self.n_dp = lax.axis_size("dp")
        self.micro, self.seqs, self.span = micro, seqs, span
        self.n_seq = micro * seqs
        self.parts = self.n_ctx // self.n_seq
        assert self.parts * self.n_seq == self.n_ctx
        self.half = span // 2
        self.sub = self.half // self.parts
        self.rows = self.n_ctx * self.sub
        self.section = lax.axis_index("section")
        self.dp = lax.axis_index("dp")
        self.ctx = lax.axis_index("ctx")
        self.staged = w_in.shape[1] % 16 == 0 and self.n_ctx == 4 and self.n_dp == 4
        self.blocks = self.n_dp if self.staged else 1
        self.shards = self.n_dp * self.n_ctx if self.staged else 1
        self.shard_rows = width // self.shards
        self.meta = jnp.stack([self.section, self.dp]).astype(jnp.int32)


X_BIT, Y_BIT = 1, 2


def other_core(value):
    return lax.ppermute(value, "section", [(0, 1), (1, 0)])


def xor_dp(plan, value, mask):
    return lax.ppermute(value, "dp", [(i, i ^ mask) for i in range(plan.n_dp)])


def xor_ctx(plan, value, mask):
    return lax.ppermute(value, "ctx", [(i, i ^ mask) for i in range(plan.n_ctx)])


def exchange_ctx(value, dim=0):
    return lax.all_to_all(value, "ctx", dim, dim, tiled=True)


def spread_ctx(plan, shard):
    return exchange_ctx(jnp.concatenate([shard] * plan.n_ctx, axis=0))


def after(value, *earlier):
    earlier = [item for item in earlier if item is not None]
    if not earlier:
        return value
    return lax.optimization_barrier((value, *earlier))[0]


class Spread:
    def __init__(self, own, relative):
        self.own, self.relative = own, relative

    def share(self, *earlier):
        self.other = other_core(after(self.own, *earlier))

    def refs(self):
        return [self.own, self.other]


def to_lanes_of_halves(tall):
    half = tall.shape[1] // 2
    return jnp.concatenate([to_lanes(tall[:, :half]), to_lanes(tall[:, half:])], axis=1)


def to_lanes(tall):
    rows = tall.shape[0] // 4
    return jnp.concatenate([tall[i * rows : (i + 1) * rows] for i in range(4)], axis=1)


def from_lanes(wide):
    cols = wide.shape[1] // 4
    return jnp.concatenate([wide[:, i * cols : (i + 1) * cols] for i in range(4)], axis=0)


def gather_natural(plan, shard, tall=0):
    gathered = lax.all_gather(shard, ("dp", "ctx"), axis=0, tiled=True)
    if plan.staged:
        return Spread(gathered.reshape(plan.shards, plan.shard_rows, -1), False)
    if tall:
        cut = gathered.shape[1] - tall
        n = plan.n_dp * plan.n_ctx
        quarters = gathered[:, cut:].reshape(n, plan.width // n, 4, tall // 4).transpose(0, 2, 1, 3)
        gathered = jnp.concatenate([gathered[:, :cut], to_lanes(quarters.reshape(-1, tall // 4))], axis=1)
    return Spread(gathered[None], False)


class SpreadDp:
    def __init__(self, plan, block, *earlier):
        self.plan = plan
        self.block = after(block, *earlier)
        self.got = [xor_dp(plan, self.block, mask) for mask in (X_BIT, Y_BIT, X_BIT | Y_BIT)]

    def result(self, *earlier):
        plan = self.plan
        blocks = jnp.stack([after(self.block, *earlier), *self.got])
        return Spread(blocks.reshape(plan.shards, plan.shard_rows, -1), True)


class Collect:
    def __init__(self, plan, blocks):
        self.plan = plan
        self.blocks = [blocks[0]] + [xor_dp(plan, blocks[mask], mask) for mask in range(1, plan.n_dp)]

    def first(self, order):
        order.need(*self.blocks[1:])

    def second(self, order):
        plan = self.plan
        own = order.gate(self.blocks[0])
        block = sum(value.astype(F32) for value in [own, *self.blocks[1:]]).astype(BF16)
        order.mark(block)
        self.parts = exchange_ctx(block.reshape(plan.n_ctx, plan.shard_rows, -1))

    def last(self, order):
        order.need(self.parts)

    def result(self):
        return jnp.sum(self.parts.astype(F32), axis=0).astype(BF16)


def smem():
    return pl.BlockSpec(memory_space=pltpu.SMEM)


def anywhere():
    return pl.BlockSpec(memory_space=pl.ANY)


def whole(shape):
    return pl.BlockSpec(shape, lambda i: (0,) * len(shape))


def rows_of(step, width):
    return pl.BlockSpec((step, width), lambda i: (i, 0))


def params(megabytes):
    return pltpu.CompilerParams(vmem_limit_bytes=megabytes * 1024 * 1024)


def cost(flops, bytes_accessed, transcendentals=0):
    return pl.CostEstimate(
        flops=int(flops * COST_SHARE),
        bytes_accessed=int(bytes_accessed * COST_SHARE),
        transcendentals=int(transcendentals * COST_SHARE),
    )


def block_copies(meta, ref, relative, place, lanes, sems, first):
    blocks = 4 if relative else 1
    count = ref.shape[0] // blocks
    copies = []
    for mask in range(blocks):
        start = (meta[1] ^ mask) * count if relative else 0
        copies.append(
            pltpu.make_async_copy(
                ref.at[pl.ds(mask * count, count), :, lanes],
                place(pl.ds(start, count)),
                sems.at[first + mask],
            )
        )
    return copies


def run(copies):
    for copy in copies:
        copy.start()


def wait(copies):
    for copy in copies:
        copy.wait()


class Loads:
    def __init__(self, section, own, other, carrier=None):
        self.section, self.own, self.other, self.carrier = section, own, other, carrier

    def each(self, act):
        if self.carrier is None:
            act(self.own)
            act(self.other)
            return
        pl.when(self.section == self.carrier)(lambda: act(self.own))
        pl.when(self.section != self.carrier)(lambda: act(self.other))

    def start(self):
        self.each(run)

    def wait(self):
        self.each(wait)


def split_refs(refs, counts):
    out, at = [], 0
    for count in counts:
        out.append(refs[at : at + count])
        at += count
    return out


def side(which, half):
    return pl.ds(pl.multiple_of(which * half, 128), half)


def load_halves(meta, relative, refs, matrix, start, sems, first):
    half = matrix.shape[-1] // 2
    lanes = slice(start, start + half)

    def at(which):
        return lambda shards: matrix.at[shards, :, side(which, half)]

    own = block_copies(meta, refs[0], relative, at(meta[0]), lanes, sems, first)
    other = block_copies(meta, refs[1], relative, at(1 - meta[0]), lanes, sems, first + 4)
    return Loads(meta[0], own, other)


def load_tall(meta, relative, refs, matrix, start, sems, first):
    half = matrix.shape[-1] // 2
    own, other = [], []
    for quarter in range(4):
        lanes = slice(start + quarter * half, start + (quarter + 1) * half)

        def at(which, quarter=quarter):
            return lambda shards: matrix.at[shards, quarter, :, side(which, half)]

        where = first + 8 * quarter
        own += block_copies(meta, refs[0], relative, at(meta[0]), lanes, sems, where)
        other += block_copies(meta, refs[1], relative, at(1 - meta[0]), lanes, sems, where + 4)
    return Loads(meta[0], own, other)


def load_one(meta, relative, refs, matrix, start, sems, first, carrier):
    lanes = slice(start, start + matrix.shape[-1])

    def at(shards):
        return matrix.at[shards]

    own = block_copies(meta, refs[0], relative, at, lanes, sems, first)
    other = block_copies(meta, refs[1], relative, at, lanes, sems, first)
    return Loads(meta[0], own, other, carrier)


def flat(matrix):
    return matrix.reshape(-1, matrix.shape[-1])


def row_step(rows, step=128):
    return step if rows % step == 0 else rows


def qkv_kernel(relative, meta, x_ref, cos_ref, sin_ref, *refs):
    attn_refs, rest = split_refs(refs, (2, len(refs) - 2))
    a_ref, q_ref, kv_ref, gains_ref, wqk, wv, columns, sems = rest
    width = wv.shape[-1]
    qk = load_halves(meta, relative, attn_refs, wqk, 0, sems, 0)
    v = load_one(meta, relative, attn_refs, wv, width, sems, 8, 0)
    gain = load_one(meta, relative, attn_refs, columns, 2 * width, sems, 12, 0)
    first = pl.program_id(0) == 0

    @pl.when(first)
    def _():
        gain.start()
        qk.start()
        v.start()
        gain.wait()
        gains_ref[...] = jnp.transpose(flat(columns[...]).astype(F32))[:8]

    normed, _ = normalise(x_ref[...].astype(F32))
    a = (normed * gains_ref[0:1, :]).astype(BF16)
    a_ref[...] = jnp.transpose(a)

    @pl.when(first)
    def _():
        qk.wait()
        v.wait()

    cos, sin = cos_ref[...], sin_ref[...]
    for which in range(2):
        out = nn(a, flat(wqk[:, :, which * width : (which + 1) * width]))
        for pair in range(width // PAIR):
            lanes = slice(pair * PAIR, (pair + 1) * PAIR)
            block = out[:, lanes]
            turned = block * cos + swap_halves(block) * sin
            if which == 0:
                q_ref[:, lanes] = (turned * HD**-0.5).astype(BF16)
            else:
                kv_ref[0, :, lanes] = turned.astype(BF16)
    kv_ref[1] = nn(a, flat(wv[...])).astype(BF16)


def qkv_forward(plan, x, cos, sin, attn):
    rows, width = x.shape
    step = row_step(rows)
    return pl.pallas_call(
        functools.partial(qkv_kernel, attn.relative),
        out_shape=[
            jax.ShapeDtypeStruct((width, rows), BF16),
            jax.ShapeDtypeStruct((rows, width), BF16),
            jax.ShapeDtypeStruct((2, rows, width), BF16),
            jax.ShapeDtypeStruct((8, width), F32),
        ],
        grid=(rows // step,),
        in_specs=[smem(), rows_of(step, width), rows_of(step, PAIR), rows_of(step, PAIR)]
        + [anywhere()] * 2,
        out_specs=[
            pl.BlockSpec((width, step), lambda i: (0, i)),
            rows_of(step, width),
            pl.BlockSpec((2, step, width), lambda i: (0, i, 0)),
            whole((8, width)),
        ],
        scratch_shapes=[
            pltpu.VMEM((plan.shards, plan.shard_rows, 2 * width), BF16),
            pltpu.VMEM((plan.shards, plan.shard_rows, width), BF16),
            pltpu.VMEM((plan.shards, plan.shard_rows, GAIN_LANES), BF16),
            pltpu.SemaphoreType.DMA((16,)),
        ],
        compiler_params=params(56),
        cost_estimate=cost(6 * rows * width * width, 12 * rows * width + 6 * width * width),
        name="qkv_forward",
    )(plan.meta, x, cos, sin, *attn.refs())


def lane_mask(shape, head):
    lane = lax.broadcasted_iota(jnp.int32, shape, 1)
    return lane < HD if head == 0 else lane >= HD


def with_ones(query):
    lane = lax.broadcasted_iota(jnp.int32, query.shape, 1)
    return jnp.concatenate([query, jnp.where(lane == 0, 1.0, 0.0).astype(BF16)], axis=1)


def attention_kernel(chunks, key_block, q_ref, *refs):
    kv = refs[:chunks]
    bias_ref, o_ref, ot_ref, lse_ref, s_scr, vt_scr = refs[chunks:]
    rows = q_ref.shape[0]
    per_chunk = rows // key_block
    query = q_ref[...]
    for c in range(chunks):
        vt_scr[:, c * rows : (c + 1) * rows] = jnp.transpose(kv[c][1])
    outs = []
    for head in range(2):
        extended = with_ones(jnp.where(lane_mask(query.shape, head), query, jnp.zeros_like(query)))
        peak = jnp.full((1, rows), -jnp.inf, F32)
        for c in range(chunks):
            for j in range(per_chunk):
                at = slice(j * key_block, (j + 1) * key_block)
                everywhere = slice(c * rows + at.start, c * rows + at.stop)
                keys = jnp.concatenate([kv[c][0, at, :], bias_ref[everywhere, :]], axis=1)
                scores = nt(keys, extended)
                s_scr[everywhere, :] = scores
                peak = jnp.maximum(peak, jnp.max(scores, axis=0, keepdims=True))
        total = jnp.zeros((1, rows), F32)
        out = jnp.zeros((PAIR, rows), F32)
        for c in range(chunks):
            for j in range(per_chunk):
                everywhere = slice(c * rows + j * key_block, c * rows + (j + 1) * key_block)
                weights = jnp.exp(s_scr[everywhere, :] - peak)
                total = total + jnp.sum(weights, axis=0, keepdims=True)
                out = out + nn(vt_scr[:, everywhere], weights.astype(BF16))
        lse_ref[0, head : head + 1, :] = peak + jnp.log(total)
        outs.append(out / total)
    row = lax.broadcasted_iota(jnp.int32, outs[0].shape, 0)
    out = jnp.where(row < HD, outs[0], outs[1])
    o_ref[...] = jnp.transpose(out).astype(BF16)
    ot_ref[...] = out.astype(BF16)


def attention_forward(plan, query, kv, bias):
    rows, width = query.shape
    chunks = len(kv)
    keys = chunks * rows
    pair_block = pl.BlockSpec((rows, PAIR), lambda p: (0, p))
    kv_block = pl.BlockSpec((2, rows, PAIR), lambda p: (0, 0, p))
    return pl.pallas_call(
        functools.partial(attention_kernel, chunks, min(256, rows)),
        out_shape=[
            jax.ShapeDtypeStruct((rows, width), BF16),
            jax.ShapeDtypeStruct((width, rows), BF16),
            jax.ShapeDtypeStruct((plan.pairs, 8, rows), F32),
        ],
        grid=(plan.pairs,),
        in_specs=[pair_block] + [kv_block] * chunks + [pl.BlockSpec((keys, PAIR), lambda p: (0, 0))],
        out_specs=[
            pair_block,
            pl.BlockSpec((PAIR, rows), lambda p: (p, 0)),
            pl.BlockSpec((1, 8, rows), lambda p: (p, 0, 0)),
        ],
        scratch_shapes=[pltpu.VMEM((keys, rows), F32), pltpu.VMEM((PAIR, keys), BF16)],
        compiler_params=params(56),
        cost_estimate=cost(
            16 * rows * keys * width, 4 * rows * width + 4 * keys * width, rows * keys * plan.heads
        ),
        name="attention_forward",
    )(query, *kv, bias)


def layer_loads(meta, relative, attn_refs, ffn_refs, wo, w1, w2, sems):
    half = w1.shape[-1] // 2
    out = load_one(meta, relative[0], attn_refs, wo, wo.shape[-1], sems, 0, 1)
    first = load_halves(meta, relative[1], ffn_refs, w1, 0, sems, 4)
    second = load_tall(meta, relative[1], ffn_refs, w2, half, sems, 12)
    return out, first, second


def layer_scratch(plan):
    width, hidden, n, rows = plan.width, plan.hidden, plan.shards, plan.shard_rows
    return [
        pltpu.VMEM((n, rows, width), BF16),
        pltpu.VMEM((n, rows, hidden), BF16),
        pltpu.VMEM((n, 4, rows, width), BF16),
        pltpu.SemaphoreType.DMA((44,)),
    ]


def tall_chunk(w2, i):
    n = w2.shape[0]
    value = w2[pl.ds(i * (n // 4), n // 4)] if n >= 4 else w2[0, i]
    return flat(value)


def ffn_kernel(relative, meta, o_ref, x_ref, gains_ref, *refs):
    attn_refs, ffn_refs, rest = split_refs(refs, (2, 2, len(refs) - 4))
    u2_ref, bt_ref, acts_ref, low_ref, ht_ref, slope_ref, wo, w1, w2, sems, b_ref = rest
    out, first, second = layer_loads(meta, relative, attn_refs, ffn_refs, wo, w1, w2, sems)
    chunk = slope_ref.shape[1]
    i = pl.program_id(0)

    @pl.when(i == 0)
    def _():
        out.start()
        first.start()
        second.start()
        out.wait()
        u2 = x_ref[...].astype(F32) + nn(o_ref[...], flat(wo[...]))
        u2_ref[...] = u2
        acts_ref[...] = u2
        b = (normalise(u2)[0] * gains_ref[1:2, :]).astype(BF16)
        b_ref[...] = b
        bt_ref[...] = jnp.transpose(b)
        first.wait()
        second.wait()

    at = pl.ds(pl.multiple_of(i * chunk, chunk), chunk)
    hp = nn(b_ref[...], flat(w1[:, :, at]))
    cdf = 0.5 * (1.0 + lax.erf(hp * (0.5**0.5)))
    density = jnp.exp(-0.5 * hp * hp) * 0.3989422804014327
    h = (hp * cdf).astype(BF16)
    ht_ref[...] = jnp.transpose(h)
    slope_ref[...] = (cdf + hp * density).astype(BF16)
    acts_ref[...] += nn(h, tall_chunk(w2, i))

    @pl.when(i == pl.num_programs(0) - 1)
    def _():
        low_ref[...] = acts_ref[...].astype(BF16)


def ffn_forward(plan, o, x, gains, attn, ffn):
    rows, width = x.shape
    hidden = plan.hidden
    chunk = hidden // 4
    refs = [*attn.refs(), *ffn.refs()]
    relative = (attn.relative, ffn.relative)
    columns = pl.BlockSpec((rows, chunk), lambda i: (0, i))
    return pl.pallas_call(
        functools.partial(ffn_kernel, relative),
        out_shape=[
            jax.ShapeDtypeStruct((rows, width), F32),
            jax.ShapeDtypeStruct((width, rows), BF16),
            jax.ShapeDtypeStruct((rows, width), F32),
            jax.ShapeDtypeStruct((rows, width), BF16),
            jax.ShapeDtypeStruct((hidden, rows), BF16),
            jax.ShapeDtypeStruct((rows, hidden), BF16),
        ],
        grid=(hidden // chunk,),
        in_specs=[smem(), whole((rows, width)), whole((rows, width)), whole((8, width))]
        + [anywhere()] * len(refs),
        out_specs=[whole((rows, width)), whole((width, rows)), whole((rows, width)), whole((rows, width))]
        + [rows_of(chunk, rows), columns],
        scratch_shapes=[
            *layer_scratch(plan),
            pltpu.VMEM((rows, width), BF16),
        ],
        compiler_params=params(56),
        cost_estimate=cost(
            4 * rows * width * hidden + 2 * rows * width * width + 60 * rows * hidden,
            20 * rows * width + 4 * rows * hidden + 4 * width * hidden,
            2 * rows * hidden,
        ),
        name="ffn_forward",
    )(plan.meta, o, x, gains, *refs)


def ffn_back_kernel(relative, meta, c_ref, slope_ref, u2_ref, gains_ref, *refs):
    attn_refs, ffn_refs, rest = split_refs(refs, (2, 2, len(refs) - 4))
    cf_ref, dhp_ref, du2_ref, dz_ref, do_ref, dg_ref, send_ref, wo, w1, w2, sems, acc = rest
    out, first, second = layer_loads(meta, relative, attn_refs, ffn_refs, wo, w1, w2, sems)
    chunk = dhp_ref.shape[1]
    i = pl.program_id(0)

    @pl.when(i == 0)
    def _():
        second.start()
        first.start()
        out.start()
        cf_ref[...] = c_ref[...].astype(BF16)
        acc[...] = jnp.zeros_like(acc)
        second.wait()
        first.wait()
        out.wait()

    at = pl.ds(pl.multiple_of(i * chunk, chunk), chunk)
    dh = nt(cf_ref[...], tall_chunk(w2, i))
    dhp = (dh * slope_ref[...].astype(F32)).astype(BF16)
    dhp_ref[...] = dhp
    there = 1 - meta[0]
    steps = pl.num_programs(0) // 2

    @pl.when(i // steps == there)
    def _():
        send_ref[:, pl.ds(pl.multiple_of((i % steps) * chunk, 128), chunk)] = dhp
    acc[...] += nt(dhp, flat(w1[:, :, at]))

    @pl.when(i == pl.num_programs(0) - 1)
    def _():
        grad, dgain = norm_back(u2_ref[...], gains_ref[1:2, :], acc[...])
        du2 = c_ref[...].astype(F32) + grad
        du2_ref[...] = du2
        dg_ref[...] = dgain
        dz = du2.astype(BF16)
        dz_ref[...] = dz
        do_ref[...] = nt(dz, flat(wo[...])).astype(BF16)
        half = dz.shape[1] // 2
        begin = send_ref.shape[1] - 2 * half
        send_ref[:, begin : begin + half] = dz_ref[:, side(there, half)]
        send_ref[:, begin + half :] = cf_ref[:, side(there, half)]


def ffn_backward(plan, c, slope, u2, gains, attn, ffn):
    rows, width = u2.shape
    hidden = plan.hidden
    chunk = hidden // 4
    refs = [*attn.refs(), *ffn.refs()]
    relative = (attn.relative, ffn.relative)
    columns = pl.BlockSpec((rows, chunk), lambda i: (0, i))
    wide = jax.ShapeDtypeStruct((rows, width), BF16)
    full = whole((rows, width))
    return pl.pallas_call(
        functools.partial(ffn_back_kernel, relative),
        out_shape=[
            wide,
            jax.ShapeDtypeStruct((rows, hidden), BF16),
            jax.ShapeDtypeStruct((rows, width), F32),
            wide,
            wide,
            jax.ShapeDtypeStruct((1, width), F32),
            jax.ShapeDtypeStruct((rows, hidden // 2 + width), BF16),
        ],
        grid=(hidden // chunk,),
        in_specs=[smem(), full, columns, full, whole((8, width))] + [anywhere()] * len(refs),
        out_specs=[full, columns, full, full, full, whole((1, width)), whole((rows, hidden // 2 + width))],
        scratch_shapes=[
            *layer_scratch(plan),
            pltpu.VMEM((rows, width), F32),
        ],
        compiler_params=params(56),
        cost_estimate=cost(
            4 * rows * width * hidden + 2 * rows * width * width,
            18 * rows * width + 4 * rows * hidden + 4 * width * hidden + 2 * width * width,
        ),
        name="ffn_backward",
    )(plan.meta, c, slope, u2, gains, *refs)


def attention_back_kernel(chunks, key_block, q_ref, do_ref, o_ref, lse_ref, bias_ref, *refs):
    kv = refs[:chunks]
    dq_ref, dk_ref, dv_ref = refs[chunks : chunks + 3]
    far = refs[chunks + 3 : 2 * chunks + 2]
    kt_scr, dk_scr, dv_scr = refs[2 * chunks + 2 :]
    rows = q_ref.shape[0]
    per_chunk = rows // key_block
    query, grad = q_ref[...], do_ref[...]
    for c in range(chunks):
        kt_scr[:, c * rows : (c + 1) * rows] = jnp.transpose(kv[c][0])
    products = jnp.transpose(grad.astype(F32) * o_ref[...].astype(F32))
    outs = []
    for head in range(2):
        mask = lane_mask(query.shape, head)
        masked_query = jnp.where(mask, query, jnp.zeros_like(query))
        masked_grad = jnp.where(mask, grad, jnp.zeros_like(grad))
        extended = with_ones(masked_query)
        delta = jnp.sum(products[head * HD : (head + 1) * HD], axis=0, keepdims=True)
        lse = lse_ref[0, head : head + 1, :]
        dqt = jnp.zeros((PAIR, rows), F32)
        for c in range(chunks):
            for j in range(per_chunk):
                at = slice(j * key_block, (j + 1) * key_block)
                everywhere = slice(c * rows + at.start, c * rows + at.stop)
                keys = jnp.concatenate([kv[c][0, at, :], bias_ref[everywhere, :]], axis=1)
                weights = jnp.exp(nt(keys, extended) - lse)
                grad_weights = nt(kv[c][1, at, :], masked_grad)
                grad_scores = (weights * (grad_weights - delta)).astype(BF16)
                dv = nn(weights.astype(BF16), masked_grad)
                dk = nn(grad_scores, masked_query)
                dqt = dqt + nn(kt_scr[:, everywhere], grad_scores)
                if head == 0:
                    dv_scr[everywhere, :] = dv
                    dk_scr[everywhere, :] = dk
                elif c == 0:
                    dk_ref[at, :] = dk_scr[everywhere, :] + dk
                    dv_ref[at, :] = dv_scr[everywhere, :] + dv
                else:
                    far[c - 1][0, at, :] = (dk_scr[everywhere, :] + dk).astype(BF16)
                    far[c - 1][1, at, :] = (dv_scr[everywhere, :] + dv).astype(BF16)
        outs.append(dqt)
    row = lax.broadcasted_iota(jnp.int32, outs[0].shape, 0)
    dq_ref[...] = jnp.transpose(jnp.where(row < HD, outs[0], outs[1])).astype(BF16)


def attention_backward(plan, query, grad, o, lse, bias, kv):
    rows, width = query.shape
    chunks = len(kv)
    keys = chunks * rows
    pair_block = pl.BlockSpec((rows, PAIR), lambda p: (0, p))
    kv_block = pl.BlockSpec((2, rows, PAIR), lambda p: (0, 0, p))
    near = jax.ShapeDtypeStruct((rows, width), F32)
    return pl.pallas_call(
        functools.partial(attention_back_kernel, chunks, min(256, rows)),
        out_shape=[jax.ShapeDtypeStruct((rows, width), BF16), near, near]
        + [jax.ShapeDtypeStruct((2, rows, width), BF16)] * (chunks - 1),
        grid=(plan.pairs,),
        in_specs=[pair_block] * 3
        + [
            pl.BlockSpec((1, 8, rows), lambda p: (p, 0, 0)),
            pl.BlockSpec((keys, PAIR), lambda p: (0, 0)),
        ]
        + [kv_block] * chunks,
        out_specs=[pair_block] * 3 + [kv_block] * (chunks - 1),
        scratch_shapes=[
            pltpu.VMEM((PAIR, keys), BF16),
            pltpu.VMEM((keys, PAIR), F32),
            pltpu.VMEM((keys, PAIR), F32),
        ],
        compiler_params=params(56),
        cost_estimate=cost(
            40 * rows * keys * width,
            16 * rows * width + 8 * keys * width,
            rows * keys * plan.heads,
        ),
        name="attention_backward",
    )(query, grad, o, lse, bias, *kv)


def qkv_back_kernel(
    spread, n_far, meta, dq_ref, dk_ref, dv_ref, du2_ref, x_ref, gains_ref, cos_ref, sin_ref, *refs
):
    far, attn_refs, rest = split_refs(refs, (n_far, len(refs) - n_far - 8, 8))
    dqkv_ref, dx_ref, low_ref, dg_ref, send_ref, wqk, wv, sems = rest
    qk = load_halves(meta, spread, attn_refs, wqk, 0, sems, 0)
    v = load_one(meta, spread, attn_refs, wv, wv.shape[-1], sems, 8, 0)
    first = pl.program_id(0) == 0

    @pl.when(first)
    def _():
        qk.start()
        v.start()
        dg_ref[...] = jnp.zeros_like(dg_ref)

    width = x_ref.shape[1]
    cos, sin = cos_ref[...], sin_ref[...]
    for pair in range(width // PAIR):
        lanes = slice(pair * PAIR, (pair + 1) * PAIR)
        dq = dq_ref[:, lanes].astype(F32) * HD**-0.5
        dk, dv = dk_ref[:, lanes], dv_ref[:, lanes]
        for part in far:
            dk = dk + part[0, :, lanes].astype(F32)
            dv = dv + part[1, :, lanes].astype(F32)
        dk = dk.astype(BF16).astype(F32)
        dqkv_ref[:, pair * PAIR : (pair + 1) * PAIR] = (dq * cos - swap_halves(dq) * sin).astype(BF16)
        at = width + pair * PAIR
        dqkv_ref[:, at : at + PAIR] = (dk * cos - swap_halves(dk) * sin).astype(BF16)
        at = 2 * width + pair * PAIR
        dqkv_ref[:, at : at + PAIR] = dv.astype(BF16)

    @pl.when(first)
    def _():
        qk.wait()
        v.wait()

    da = nt(dqkv_ref[:, : 2 * width], flat(wqk[...]))
    da = da + nt(dqkv_ref[:, 2 * width :], flat(wv[...]))
    grad, dgain = norm_back(x_ref[...].astype(F32), gains_ref[0:1, :], da)
    dx = du2_ref[...] + grad
    dx_ref[...] = dx
    low_ref[...] = dx.astype(BF16)
    dg_ref[...] += dgain
    there = 1 - meta[0]
    wide = 3 * width // 2
    send_ref[:, :wide] = dqkv_ref[:, side(there, wide)]
    if send_ref.shape[1] > wide:
        send_ref[:, wide:] = low_ref[:, side(there, width // 2)]


def qkv_backward(plan, dq, dk, dv, far, du2, x, gains, cos, sin, attn, sent):
    rows, width = x.shape
    step = row_step(rows)
    refs = attn.refs()
    some = rows_of(step, width)
    return pl.pallas_call(
        functools.partial(qkv_back_kernel, attn.relative, len(far)),
        out_shape=[
            jax.ShapeDtypeStruct((rows, 3 * width), BF16),
            jax.ShapeDtypeStruct((rows, width), F32),
            jax.ShapeDtypeStruct((rows, width), BF16),
            jax.ShapeDtypeStruct((1, width), F32),
            jax.ShapeDtypeStruct((rows, sent), BF16),
        ],
        grid=(rows // step,),
        in_specs=[smem()]
        + [some] * 5
        + [whole((8, width)), rows_of(step, PAIR), rows_of(step, PAIR)]
        + [pl.BlockSpec((2, step, width), lambda i: (0, i, 0))] * len(far)
        + [anywhere()] * len(refs),
        out_specs=[rows_of(step, 3 * width), some, some, whole((1, width)), rows_of(step, sent)],
        scratch_shapes=[
            pltpu.VMEM((plan.shards, plan.shard_rows, 2 * width), BF16),
            pltpu.VMEM((plan.shards, plan.shard_rows, width), BF16),
            pltpu.SemaphoreType.DMA((12,)),
        ],
        compiler_params=params(56),
        cost_estimate=cost(6 * rows * width * width, 30 * rows * width + 6 * width * width),
        name="qkv_backward",
    )(plan.meta, dq, dk, dv, du2, x, gains, cos, sin, *far, *refs)


class Job:
    def __init__(self, left, right, cols, at=0, tall=False):
        self.left, self.right, self.cols, self.at, self.tall = left, right, cols, at, tall
        self.lanes = 4 * cols if tall else cols


def weight_kernel(jobs, n_lefts, n_rights, relative, meta, *refs):
    lefts, rights, (got,), outs, (acc,) = split_refs(
        refs, (n_lefts, n_rights, 1, len(refs) - n_lefts - n_rights - 2, 1)
    )
    step = pl.program_id(0)
    shards, size = acc.shape[:2]
    lane = 0
    for job in jobs:
        own, other = lefts[job.left], lefts[job.left + 1]
        if job.right is None:
            product = own[...] + other[...]
        else:
            columns = rights[job.right][:, side(meta[0], rights[job.right].shape[1] // 2)]
            product = nn(own[...], columns)
            product = product + nn(other[...], got[:, job.at : job.at + job.cols])
        if job.tall:
            product = product.reshape(shards, 4, size, job.cols)
            for quarter in range(4):
                acc[:, :, lane : lane + job.cols] = product[:, quarter]
                lane += job.cols
        else:
            acc[:, :, lane : lane + job.cols] = product.reshape(shards, size, job.cols)
            lane += job.cols
    if not relative:
        outs[0][0] = acc[...].astype(BF16)
        return
    for mask, out in enumerate(outs):

        @pl.when(step == mask)
        def _(out=out):
            out[...] = acc[...].astype(BF16)


def weight_call(plan, lefts, rights, jobs, got, relative):
    rows = rights[0].shape[0]
    n = plan.blocks
    shape = (plan.shards // n, plan.shard_rows, sum(job.lanes for job in jobs))
    if relative:
        out_shape = [jax.ShapeDtypeStruct(shape, BF16)] * n
        out_specs = [pl.BlockSpec(shape, lambda i, meta: (0, 0, 0))] * n
    else:
        out_shape = [jax.ShapeDtypeStruct((n, *shape), BF16)]
        out_specs = [pl.BlockSpec((1, *shape), lambda i, meta: (i, 0, 0, 0))]

    def block_of(i, meta):
        return (meta[1] ^ i if relative else i, 0)

    def all_of(value):
        return pl.BlockSpec(value.shape, lambda i, meta: (0, 0))

    moved = sum(value.size * 2 for value in [*lefts, *rights, got])
    moved += 2 * n * shape[0] * shape[1] * shape[2]
    flops = sum(
        4 * rows * lefts[job.left].shape[0] * job.cols for job in jobs if job.right is not None
    )
    result = pl.pallas_call(
        functools.partial(weight_kernel, jobs, len(lefts), len(rights), relative),
        out_shape=out_shape,
        grid_spec=pltpu.PrefetchScalarGridSpec(
            num_scalar_prefetch=1,
            grid=(n,),
            in_specs=[
                pl.BlockSpec((value.shape[0] // n, value.shape[1]), block_of) for value in lefts
            ]
            + [all_of(value) for value in [*rights, got]],
            out_specs=out_specs,
            scratch_shapes=[pltpu.VMEM(shape, F32)],
        ),
        compiler_params=params(56),
        cost_estimate=cost(flops, moved),
        name="weight_grads",
    )(plan.meta, *lefts, *rights, got)
    return result if relative else result[0]


class WeightGrads:
    def __init__(self, plan, order, lefts, rights, jobs, got, ahead=None):
        self.plan, self.relative = plan, plan.staged
        lefts = [order.gate(lefts[0]), *lefts[1:]]
        out = weight_call(plan, lefts, rights, jobs, got, self.relative)
        if self.relative:
            order.mark(out[0])
            earlier = ahead.sums.blocks[1:] if ahead else []
            self.sums = Collect(plan, [after(block, *earlier) for block in out])
            return
        order.mark(out)
        tall = sum(job.lanes for job in jobs if job.tall)
        out = out.reshape(plan.width, -1)
        cut = out.shape[1] - tall
        self.total = lax.psum_scatter(out[:, :cut], ("dp", "ctx"), scatter_dimension=0, tiled=True)
        if tall:
            part = from_lanes(out[:, cut:])
            part = lax.psum_scatter(part, ("dp", "ctx"), scatter_dimension=0, tiled=True)
            self.total = jnp.concatenate([self.total, to_lanes(part)], axis=1)

    def step(self, name, order):
        if self.relative:
            getattr(self.sums, name)(order)

    def result(self):
        return self.sums.result() if self.relative else self.total


class Order:
    def __init__(self):
        self.earlier = []

    def gate(self, value):
        return after(value, *self.earlier)

    def mark(self, value):
        self.earlier = [] if value is None else [value]

    def need(self, *values):
        self.earlier += [value for value in values if value is not None]


def by_section(plan, first, second):
    return jnp.where(plan.section == 0, first, second)


def take_half(plan, matrix, which):
    half = matrix.shape[-1] // 2
    return lax.dynamic_slice_in_dim(matrix, which * half, half, axis=matrix.ndim - 1)


def to_sequences(plan, tokens):
    pieces = tokens.reshape(plan.n_seq, 2, plan.half, plan.width)
    mine = lax.dynamic_index_in_dim(pieces, plan.section, 1, keepdims=False)
    mine = mine.reshape(plan.n_ctx, plan.sub, plan.width)
    return exchange_ctx(mine).reshape(plan.rows, plan.width)


def from_sequences(plan, stack):
    return exchange_ctx(stack.reshape(stack.shape[0], plan.n_ctx, plan.sub, plan.width), 1)


def arranged(plan, moved, *earlier):
    moved = after(moved, *earlier)
    return moved.reshape(moved.shape[0], plan.n_seq, plan.half, plan.width)


def to_output(plan, layers):
    own = by_section(plan, layers[0], layers[1])
    got = other_core(by_section(plan, layers[1], layers[0]))
    first = by_section(plan, own, got)
    second = by_section(plan, got, own)
    both = jnp.concatenate([first.astype(F32), second.astype(F32)], axis=1)
    return both.reshape(1, plan.micro, plan.seqs, plan.span, plan.width)


def shared_keys(plan, own):
    chunks = []
    for mask in range(plan.parts):
        here = own if mask == 0 else xor_ctx(plan, own, mask)
        chunks += [here, other_core(here)]
    return chunks


def return_keys(plan, far):
    got = []
    for mask in range(plan.parts):
        for core in range(2):
            index = 2 * mask + core
            if index == 0:
                continue
            part = far[index - 1]
            if core:
                part = other_core(part)
            if mask:
                part = xor_ctx(plan, part, mask)
            got.append(part)
    return got


def positions_of(plan, section, ctx):
    part = ctx % plan.parts
    start = jnp.arange(plan.n_ctx)[:, None] * plan.span + section * plan.half + part * plan.sub
    return (start + jnp.arange(plan.sub)[None, :]).reshape(-1)


def rope_tables(positions):
    half_width = HD // 2
    frequency = jnp.power(10000.0, -(jnp.arange(half_width).astype(F32) * 2.0) / HD)
    angles = positions.astype(F32)[:, None] * frequency[None, :]
    cos, sin = jnp.cos(angles), jnp.sin(angles)
    return jnp.concatenate([cos] * 4, axis=1), jnp.concatenate([-sin, sin, -sin, sin], axis=1)


def local(tokens, upstream, lengths, w_qkv, w_out, w_in, w_back, gain_attn, gain_ffn):
    plan = Plan(tokens, w_in)
    width = plan.width
    layers = 2

    qkv_low, out_low = w_qkv[0].astype(BF16), w_out[0].astype(BF16)
    in_low, back_low = w_in[0].astype(BF16), to_lanes_of_halves(w_back[0].astype(BF16))
    both = jnp.stack([gain_attn[0], gain_ffn[0]], axis=1).astype(BF16)
    both = jnp.pad(both, ((0, 0), (0, GAIN_LANES - 2)))
    here, there = plan.section, 1 - plan.section

    def attn_half(which):
        value = jnp.where(which == 0, qkv_low[:, 2 * width :], out_low)
        return jnp.concatenate([take_half(plan, qkv_low[:, : 2 * width], which), value, both], axis=1)

    def ffn_half(which):
        return jnp.concatenate(
            [take_half(plan, in_low, which), take_half(plan, back_low, which)], axis=1
        )

    def shards_of(half):
        kept, got = half(here), other_core(half(there))
        return by_section(plan, kept, got), by_section(plan, got, kept)

    attn_shards, ffn_shards = shards_of(attn_half), shards_of(ffn_half)
    tall = 4 * (width // 2)
    if plan.staged:
        attn0_z = spread_ctx(plan, attn_shards[0])
        attn0_dp = SpreadDp(plan, attn0_z)
        ffn0_z = spread_ctx(plan, after(ffn_shards[0], attn0_z))
        source = to_sequences(plan, after(tokens, ffn0_z))
        attn1 = gather_natural(plan, after(attn_shards[1], attn0_z), tall)
        attn0 = attn0_dp.result(ffn0_z)
        ffn0_dp = SpreadDp(plan, ffn0_z, *attn0_dp.got)
        ffn1 = gather_natural(plan, after(ffn_shards[1], attn0_z), tall)
    else:
        source = to_sequences(plan, tokens)
        attn0, attn1 = (gather_natural(plan, shard) for shard in attn_shards)
        ffn0, ffn1 = (gather_natural(plan, shard, tall) for shard in ffn_shards)
    attn0.share()

    cos, sin = rope_tables(positions_of(plan, plan.section, plan.ctx))
    sequence = plan.ctx // plan.parts
    length = lax.dynamic_index_in_dim(lengths.reshape(-1), sequence, 0, keepdims=False)
    places = []
    for mask in range(plan.parts):
        for core in range(2):
            places.append(positions_of(plan, plan.section ^ core, plan.ctx ^ mask))
    hidden_key = jnp.where(jnp.concatenate(places) < length, 0.0, MASKED)
    lane = jnp.arange(PAIR)
    bias = jnp.where(lane[None, :] == 0, hidden_key[:, None], 0.0).astype(BF16)

    order = Order()
    saved, acts, gains, others = [], [], [], []

    def forward_qkv(x, attn):
        a, query, own_kv, rows = qkv_forward(plan, order.gate(x), cos, sin, attn)
        order.mark(query)
        gains.append(rows)
        return a, query, shared_keys(plan, own_kv)

    def forward_attention(query, kv):
        out = attention_forward(plan, order.gate(query), kv, bias)
        order.mark(out[2])
        return out

    def forward_ffn(x, layer, attn, ffn, held):
        a, query, kv, o, ot, lse = held
        u2, b, result, low, h, slope = ffn_forward(
            plan, order.gate(o), x, gains[layer], attn, ffn
        )
        order.mark(low)
        saved.append((x, a, query, kv, o, ot, lse, u2, b, h, slope))
        acts.append(low)
        others.append([other_core(value) for value in (a, ot, b, h)])
        return result

    if plan.staged:
        order.need(*ffn0_dp.got[:2])
    held = forward_qkv(source, attn0)
    held += tuple(forward_attention(*held[1:]))
    if plan.staged:
        ffn0 = ffn0_dp.result(held[5])
    ffn0.share(held[5])
    attn1.share(held[5])
    x = forward_ffn(source, 0, attn0, ffn0, held)
    held = forward_qkv(x, attn1)
    held += tuple(forward_attention(*held[1:]))
    ffn1.share(held[5])
    cotangent = to_sequences(plan, after(upstream, held[1]))
    forward_ffn(x, 1, attn1, ffn1, held)
    weights = [(attn0, ffn0), (attn1, ffn1)]

    hidden_half, width_half = plan.hidden // 2, width // 2
    grads, dgains = [None] * layers, [None] * layers

    def ffn_part(layer, c):
        attn, ffn = weights[layer]
        u2, _, _, slope = saved[layer][7:]
        out = ffn_backward(plan, order.gate(c), slope, u2, gains[layer], attn, ffn)
        order.mark(out[5])
        return out

    def attention_part(layer, do):
        x, a, query, kv, o, ot, lse, u2, b, h, slope = saved[layer]
        dq, dk, dv, *far = attention_backward(plan, query, order.gate(do), o, lse, bias, kv)
        order.mark(dq)
        return dq, dk, dv, return_keys(plan, far)

    def qkv_part(layer, dq, dk, dv, far, du2, dg2):
        x = saved[layer][0]
        dqkv, dx, low, dg1, send = qkv_backward(
            plan, order.gate(dq), dk, dv, far, du2, x, gains[layer], cos, sin, weights[layer][0], wide + layer * width_half
        )
        order.mark(dg1)
        grads[layer] = low
        dgains[layer] = (dg1, dg2)
        return dqkv, dx, low, send

    wide = 3 * width // 2
    a1, ot1, b1, h1 = (saved[1][i] for i in (1, 5, 8, 9))
    a0, ot0, b0, h0 = (saved[0][i] for i in (1, 5, 8, 9))
    (far_a0, far_ot0, far_b0, far_h0), (far_a1, far_ot1, far_b1, far_h1) = others

    cf, dhp, du2, dz, do, dg2, send = ffn_part(1, cotangent)
    got = other_core(send)
    acts_back = from_sequences(plan, jnp.stack(acts))
    back = attention_part(1, do)
    sum_ffn1 = WeightGrads(
        plan,
        order,
        [b1, far_b1, ot1, far_ot1, h1, far_h1],
        [dhp, dz, cf],
        [
            Job(0, 0, hidden_half),
            Job(2, 1, width_half, hidden_half),
            Job(4, 2, width_half, hidden_half + width_half, tall=True),
        ],
        got,
    )
    order.need(acts_back)
    dqkv, c, low, send = qkv_part(1, *back, du2, dg2)
    got = other_core(send)
    grads1_back = from_sequences(plan, grads[1][None])
    cf, dhp, du2, dz, do, dg2, send = ffn_part(0, c)
    got_ffn = other_core(send)
    sum_ffn1.step("first", order)
    order.need(grads1_back)
    sum_ffn1.step("second", order)
    sum_mixed = WeightGrads(
        plan,
        order,
        [a1, far_a1, h0, far_h0],
        [dqkv, low],
        [Job(0, 0, wide), Job(2, 1, width_half, wide, tall=True)],
        got,
    )
    sum_in0 = WeightGrads(
        plan,
        order,
        [b0, far_b0, ot0, far_ot0],
        [dhp, dz],
        [Job(0, 0, hidden_half), Job(2, 1, width_half, hidden_half)],
        got_ffn,
        sum_mixed,
    )
    back = attention_part(0, do)
    sum_mixed.step("first", order)
    sum_mixed.step("second", order)
    dqkv, c, low, send = qkv_part(0, *back, du2, dg2)
    got = other_core(send)
    rows = jnp.concatenate([row for pair in dgains for row in pair], axis=0)
    columns = jnp.pad(rows.T, ((0, 0), (0, GAIN_LANES - 2 * layers)))
    sum_in0.step("first", order)
    sum_qkv0 = WeightGrads(
        plan,
        order,
        [a0, far_a0, columns, other_core(columns)],
        [dqkv],
        [Job(0, 0, wide), Job(2, None, GAIN_LANES)],
        got,
    )
    sum_in0.step("second", order)
    grads0_back = from_sequences(plan, order.gate(grads[0])[None])
    acts_back = arranged(plan, acts_back, *order.earlier)
    acts_out = to_output(plan, acts_back)
    sum_qkv0.step("second", order)
    grads0_back = arranged(plan, grads0_back, *order.earlier)
    grads1_back = arranged(plan, grads1_back, *order.earlier)

    cut = hidden_half + width_half
    ffn1_sum, mixed_sum = sum_ffn1.result(), sum_mixed.result()
    in0_sum, qkv0_sum = sum_in0.result(), sum_qkv0.result()
    gain_sums = lax.dynamic_slice_in_dim(qkv0_sum[:, wide:], plan.section * 2, 2, axis=1).T.astype(F32)
    sums = [
        (qkv0_sum[:, :wide], in0_sum[:, hidden_half:], in0_sum[:, :hidden_half], from_lanes(mixed_sum[:, wide:])),
        (
            mixed_sum[:, :wide],
            ffn1_sum[:, hidden_half:cut],
            ffn1_sum[:, :hidden_half],
            from_lanes(ffn1_sum[:, cut:]),
        ),
    ]

    def to_owner(first, second):
        own = by_section(plan, first, second)
        got = other_core(by_section(plan, second, first))
        left, right = by_section(plan, own, got), by_section(plan, got, own)
        return jnp.concatenate([left, right], axis=1).astype(F32)[None]

    weight_grads = [to_owner(one, two) for one, two in zip(*sums)]
    return (
        acts_out,
        to_output(plan, [grads0_back[0], grads1_back[0]]),
        *weight_grads,
        gain_sums[0:1],
        gain_sums[1:2],
    )


def solution(mesh):
    rows = P(None, "dp", "ctx", None)
    weight = P("section", ("dp", "ctx"), None)
    gain = P("section", ("dp", "ctx"))
    out_rows = P("section", None, "dp", "ctx", None)
    return jax.shard_map(
        local,
        mesh=mesh,
        in_specs=(rows, rows, P(None, "dp"), weight, weight, weight, weight, gain, gain),
        out_specs=(out_rows, out_rows, weight, weight, weight, weight, gain, gain),
        check_vma=False,
    )
```
